32 devices in a mesh: fsdp: 8 (over z, x), tp: 4 (over y, core).
Axes of the slice: x: 2, y: 2, z: 4, core: 2. Of those that a mesh axis runs over, the one named last changes fastest.
Arguments:
- tokens: bfloat16 [1024, 4096], P('fsdp'), may hold values from -6 to 6
- gate_left: bfloat16 [4096, 1024], P('fsdp', 'tp'), may hold values from -0.09375 to 0.09375
- gate_right: bfloat16 [1024, 14336], P('fsdp', 'tp'), may hold values from -0.1875 to 0.1875
- gate_values: bfloat16 [108, 16384], P('tp', 'fsdp'), may hold values from -0.5 to 0.5
- gate_rows: int32 [108], P('tp'), may hold values from 0 to 31
- gate_cols: int32 [108], P('tp'), may hold values from 0 to 111, as said below
- up_left: bfloat16 [4096, 1024], P('fsdp', 'tp'), may hold values from -0.09375 to 0.09375
- up_right: bfloat16 [1024, 14336], P('fsdp', 'tp'), may hold values from -0.1875 to 0.1875
- up_values: bfloat16 [108, 16384], P('tp', 'fsdp'), may hold values from -0.5 to 0.5
- up_rows: int32 [108], P('tp'), may hold values from 0 to 31
- up_cols: int32 [108], P('tp'), may hold values from 0 to 111, as said below
- grad_hidden: bfloat16 [1024, 14336], P('fsdp', 'tp'), may hold values from -6 to 6
Outputs:
- hidden: bfloat16 [1024, 14336], P('fsdp', 'tp')
- grad_gate_values: float32 [108, 16384], P('tp', 'fsdp')
- grad_up_values: float32 [108, 16384], P('tp', 'fsdp')
The draws below stay inside these ranges and needn't reach their ends.
Inputs may be any that keep to these rules, and one draw needn't show every extreme that they name: `gate_cols`: support blocks of one projection are distinct (row block, column block) pairs; the entries that lie on index t of tp have column blocks from t * 14336 // (128 * 4) to (t + 1) * 14336 // (128 * 4) - 1. Rows and columns of one projection go together. `up_cols`: as for the gate projection.
All inputs are finite; a program needn't handle non-finite values.
Results may differ from the reference program's by a relative error of at most 0.005.
Values may be sent and summed in bfloat16 or wider, within the bound.
No kernel may reach another device: no remote copies, remote signals or barrier semaphores. Data moves between devices by JAX's collectives and lax.ppermute only.
A program may use at most 128 MiB of HBM per device.

```python
import jax
import jax.numpy as jnp
from jax import lax

D = 4096
FF = 14336
R = 1024
BLK = 128
BLK_TP = 27
TOKENS = 1024
NBLK = 108
N_TP = 4


def support_cells(key):
    row_blocks = D // BLK
    col_blocks = FF // BLK // N_TP

    def one(device):
        shuffled = jax.random.permutation(jax.random.fold_in(key, device), row_blocks * col_blocks)[:BLK_TP]
        return (shuffled // col_blocks, device * col_blocks + shuffled % col_blocks)
    rows, cols = jax.vmap(one)(jnp.arange(N_TP))
    return (rows.reshape(-1).astype(jnp.int32), cols.reshape(-1).astype(jnp.int32))


def draw_gate_rows(key, part):
    return support_cells(jax.random.fold_in(key, 11))[0]


def draw_gate_cols(key, part):
    return support_cells(jax.random.fold_in(key, 11))[1]


def draw_up_rows(key, part):
    return support_cells(jax.random.fold_in(key, 12))[0]


def draw_up_cols(key, part):
    return support_cells(jax.random.fold_in(key, 12))[1]


def levels(key, shape, shards, least, high):
    level = 1.0
    for dim, blocks in shards:
        heights = jax.random.uniform(jax.random.fold_in(jax.random.fold_in(key, 6), dim), (blocks,), jnp.float32, least / len(shards), high / len(shards))
        level = level * jnp.repeat(jnp.exp(heights), shape[dim] // blocks).reshape((-1,) + (1,) * (len(shape) - 1 - dim))
    return level


def bell_draw(rng, extent, spread, reach, cuts=(), dtype=jnp.bfloat16):
    values = jax.random.normal(rng, extent, jnp.float32) * spread
    if len(cuts) > 0:
        values = levels(rng, extent, cuts, -0.22, 0.18) * values
    return jnp.clip(values, min=-reach, max=reach).astype(dtype)


def setup_inputs(seed: int = 0) -> dict:
    splits = jax.random.split(jax.random.key(seed), 13)
    tokens = bell_draw(splits[0], (TOKENS, D), 1.0, 6.0, ((0, 8),))
    gate_left = bell_draw(splits[1], (D, R), D ** -0.5, 0.09375, ((0, 8), (1, 4)))
    gate_right = bell_draw(splits[2], (R, FF), R ** -0.5, 0.1875, ((0, 8), (1, 4)))
    gate_values = bell_draw(splits[3], (NBLK, BLK * BLK), BLK ** -0.5, 0.5, ((0, 4), (1, 8)))
    gate_rows = draw_gate_rows(jax.random.fold_in(splits[12], 71), 0)
    gate_cols = draw_gate_cols(jax.random.fold_in(splits[12], 71), 0)
    up_left = bell_draw(splits[6], (D, R), D ** -0.5, 0.09375, ((0, 8), (1, 4)))
    up_right = bell_draw(splits[7], (R, FF), R ** -0.5, 0.1875, ((0, 8), (1, 4)))
    up_values = bell_draw(splits[8], (NBLK, BLK * BLK), BLK ** -0.5, 0.5, ((0, 4), (1, 8)))
    up_rows = draw_up_rows(jax.random.fold_in(splits[12], 71), 0)
    up_cols = draw_up_cols(jax.random.fold_in(splits[12], 71), 0)
    grad_hidden = bell_draw(splits[11], (TOKENS, FF), 1.0, 6.0, ((0, 8), (1, 4)))
    return dict(tokens=tokens, gate_left=gate_left, gate_right=gate_right, gate_values=gate_values, gate_rows=gate_rows, gate_cols=gate_cols, up_left=up_left, up_right=up_right, up_values=up_values, up_rows=up_rows, up_cols=up_cols, grad_hidden=grad_hidden)


def add_support(source_all, values, rows, cols, total):
    def step(index, acc):
        block = values[index].reshape(BLK, BLK)
        source = lax.dynamic_slice_in_dim(source_all, rows[index] * BLK, BLK, 1)
        start = cols[index] * BLK
        current = lax.dynamic_slice_in_dim(acc, start, BLK, 1)
        update = current + jnp.dot(source, block, preferred_element_type=jnp.float32)
        return lax.dynamic_update_slice_in_dim(acc, update, start, 1)
    return lax.fori_loop(0, values.shape[0], step, total)


def value_grads(tokens, grad_all, rows, cols):
    def one(index):
        left = lax.dynamic_slice_in_dim(tokens, rows[index] * BLK, BLK, 1)
        right = lax.dynamic_slice_in_dim(grad_all, cols[index] * BLK, BLK, 1)
        return jnp.dot(left.T, right, preferred_element_type=jnp.float32).reshape(BLK * BLK)
    return lax.map(one, jnp.arange(rows.shape[0]))


def reference(tokens, gate_left, gate_right, gate_values, gate_rows, gate_cols, up_left, up_right, up_values, up_rows, up_cols, grad_hidden):
    rank_gate = jnp.dot(tokens, gate_left, preferred_element_type=jnp.float32).astype(jnp.bfloat16)
    rank_up = jnp.dot(tokens, up_left, preferred_element_type=jnp.float32).astype(jnp.bfloat16)
    pre_gate = jnp.dot(rank_gate, gate_right, preferred_element_type=jnp.float32)
    pre_gate = add_support(tokens, gate_values, gate_rows, gate_cols, pre_gate)
    pre_up = jnp.dot(rank_up, up_right, preferred_element_type=jnp.float32)
    pre_up = add_support(tokens, up_values, up_rows, up_cols, pre_up)
    sigma = jax.nn.sigmoid(pre_gate)
    silu = pre_gate * sigma
    hidden = (silu * pre_up).astype(jnp.bfloat16)
    upstream = grad_hidden.astype(jnp.float32)
    dpre_gate = (upstream * pre_up * sigma * (1.0 + pre_gate * (1.0 - sigma))).astype(jnp.bfloat16)
    dpre_up = (upstream * silu).astype(jnp.bfloat16)
    grad_gate_values = value_grads(tokens, dpre_gate, gate_rows, gate_cols)
    grad_up_values = value_grads(tokens, dpre_up, up_rows, up_cols)
    return hidden, grad_gate_values, grad_up_values
```

```python
import functools

import jax
import jax.numpy as jnp
from jax import lax
from jax.experimental import pallas as pl
from jax.experimental.pallas import tpu as pltpu
from jax.sharding import PartitionSpec as P

BLK = 128


def support_forward(tokens, blocks, rows, cols_local, col_blocks):
    width = tokens.shape[1] // BLK
    sources = tokens.reshape(tokens.shape[0], width, BLK)[:, rows, :]
    parts = jnp.einsum("tkb,kbc->tkc", sources, blocks, preferred_element_type=jnp.float32)
    placed = (
        jnp.zeros((tokens.shape[0], col_blocks, BLK), jnp.float32).at[:, cols_local, :].add(parts)
    )
    return (placed.reshape(tokens.shape[0], col_blocks * BLK), sources)


def value_terms(sources_gate, dpre_gate, local_gate, sources_up, dpre_up, local_up, col_blocks):
    picked_gate = dpre_gate.reshape(dpre_gate.shape[0], col_blocks, BLK)[:, local_gate, :]
    picked_up = dpre_up.reshape(dpre_up.shape[0], col_blocks, BLK)[:, local_up, :]
    value_gate = jnp.einsum(
        "tkb,tkc->kbc", sources_gate, picked_gate, preferred_element_type=jnp.float32
    )
    value_up = jnp.einsum("tkb,tkc->kbc", sources_up, picked_up, preferred_element_type=jnp.float32)
    return (
        value_gate.reshape(value_gate.shape[0], BLK * BLK),
        value_up.reshape(value_up.shape[0], BLK * BLK),
    )


def on_device(
    tokens,
    gate_left,
    gate_right,
    gate_values,
    gate_rows,
    gate_cols,
    up_left,
    up_right,
    up_values,
    up_rows,
    up_cols,
    grad_hidden,
):
    left_gate, left_up = (
        lax.all_gather(gate_left, "fsdp", axis=0, tiled=True),
        lax.all_gather(up_left, "fsdp", axis=0, tiled=True),
    )
    rank_gate = jnp.dot(tokens, left_gate, preferred_element_type=jnp.float32).astype(jnp.bfloat16)
    rank_up = jnp.dot(tokens, left_up, preferred_element_type=jnp.float32).astype(jnp.bfloat16)
    full_gate, full_up = (
        lax.all_gather(rank_gate, "tp", axis=1, tiled=True),
        lax.all_gather(rank_up, "tp", axis=1, tiled=True),
    )
    flat_gate, flat_up = (
        lax.all_gather(gate_values, "fsdp", axis=1, tiled=True),
        lax.all_gather(up_values, "fsdp", axis=1, tiled=True),
    )
    blocks_gate = flat_gate.reshape(flat_gate.shape[0], BLK, BLK)
    blocks_up = flat_up.reshape(flat_up.shape[0], BLK, BLK)
    right_gate = lax.all_gather(gate_right, "fsdp", axis=0, tiled=True)
    right_up = lax.all_gather(up_right, "fsdp", axis=0, tiled=True)
    col_blocks = right_gate.shape[1] // BLK
    col_base = lax.axis_index("tp") * col_blocks
    local_gate = gate_cols - col_base
    local_up = up_cols - col_base
    sparse_gate, sources_gate = support_forward(
        tokens, blocks_gate, gate_rows, local_gate, col_blocks
    )
    sparse_up, sources_up = support_forward(tokens, blocks_up, up_rows, local_up, col_blocks)
    pre_gate = jnp.dot(full_gate, right_gate, preferred_element_type=jnp.float32) + sparse_gate
    pre_up = jnp.dot(full_up, right_up, preferred_element_type=jnp.float32) + sparse_up
    sigma = jax.nn.sigmoid(pre_gate)
    silu = pre_gate * sigma
    upstream = grad_hidden.astype(jnp.float32)
    dpre_gate = (upstream * pre_up * sigma * (1.0 + pre_gate * (1.0 - sigma))).astype(jnp.bfloat16)
    dpre_up = (upstream * silu).astype(jnp.bfloat16)
    hidden = (silu * pre_up).astype(jnp.bfloat16)
    value_gate, value_up = value_terms(
        sources_gate, dpre_gate, local_gate, sources_up, dpre_up, local_up, col_blocks
    )
    grad_gate_values, grad_up_values = (
        lax.psum_scatter(value_gate, "fsdp", scatter_dimension=1, tiled=True),
        lax.psum_scatter(value_up, "fsdp", scatter_dimension=1, tiled=True),
    )
    return (hidden, grad_gate_values, grad_up_values)


ANY = pl.BlockSpec(memory_space=pl.ANY)
VMEM = pl.BlockSpec(memory_space=pltpu.VMEM)
SMEM = pl.BlockSpec(memory_space=pltpu.SMEM)
BF16, F32 = jnp.bfloat16, jnp.float32


def at(start, size):
    return pl.ds(pl.multiple_of(start, BLK), size)


def run_copies(pairs, sems):
    copies = [pltpu.make_async_copy(s, d, sems.at[i]) for i, (s, d) in enumerate(pairs)]
    for copy in copies:
        copy.start()
    return copies


def partial_kernel(nz, idx, tokens, *refs):
    mine, other = refs[: nz - 1], refs[nz - 1 : 2 * nz - 2]
    left_g, left_u, recv_g, recv_u = refs[2 * nz - 2 : 2 * nz + 2]
    own_out, outs = refs[2 * nz + 2], refs[2 * nz + 3 : 3 * nz + 2]
    left, toks, sems = refs[3 * nz + 2 :]
    z, x, c = idx[0], idx[1], idx[2]
    depth, width = left_g.shape
    pairs = [
        (left_g, left.at[x, :, pl.ds(0, width)]),
        (left_u, left.at[x, :, pl.ds(width, width)]),
        (recv_g, left.at[1 - x, :, pl.ds(0, width)]),
        (recv_u, left.at[1 - x, :, pl.ds(width, width)]),
        (tokens.at[:, at(z * 2 * depth, 2 * depth)], toks.at[0]),
    ]
    for j in range(1, nz):
        pairs.append((mine[j - 1], toks.at[j, :, at(c * depth, depth)]))
        pairs.append((other[j - 1], toks.at[j, :, at((1 - c) * depth, depth)]))
    for copy in run_copies(pairs, sems):
        copy.wait()
    weights = left[...].reshape(2 * depth, 2 * width)
    rows = toks.shape[1]
    total = jnp.dot(
        toks[...].reshape(nz * rows, 2 * depth), weights, preferred_element_type=F32
    )
    own_out[...] = total[:rows]
    for j in range(1, nz):
        outs[j - 1][...] = total[j * rows : (j + 1) * rows].astype(BF16)


def lowrank_kernel(nf, nt, idx, *refs):
    ranks, rights = refs[:nt], refs[nt : nt + nf]
    outs = refs[nt + nf : nt + 2 * nf]
    rank, weight, sems = refs[nt + 2 * nf :]
    f, t = idx[3], idx[4]
    pairs = [(ranks[s], rank.at[t ^ s]) for s in range(nt)]
    pairs += [(rights[k], weight.at[f ^ k]) for k in range(nf)]
    for copy in run_copies(pairs, sems):
        copy.wait()
    rows, width = rank.shape[2], rank.shape[3]
    cols = weight.shape[2]
    weights = weight[...].reshape(nt, width, cols)
    group = min(4, nf)
    for m in range(0, nf, group):
        total = None
        for s in range(nt):
            lhs = rank[s, m : m + group].reshape(group * rows, width)
            part = jnp.dot(lhs, weights[s], preferred_element_type=F32)
            total = part if total is None else total + part
        for i in range(group):
            outs[m + i][...] = total[i * rows : (i + 1) * rows].astype(BF16)


def sparse_kernel(nf, idx, gate_rows, gate_cols, up_rows, up_cols, tokens, *refs):
    values, out, blocks, sems = refs[:nf], refs[nf], refs[nf + 1], refs[nf + 2]
    f = idx[3]
    copies = run_copies([(values[k], blocks.at[:, f ^ k]) for k in range(nf)], sems)
    out[...] = jnp.zeros_like(out)
    for copy in copies:
        copy.wait()
    count = gate_rows.shape[0]
    for p, (rows, cols) in enumerate(((gate_rows, gate_cols), (up_rows, up_cols))):

        def step(k, carry, p=p, rows=rows, cols=cols):
            source = tokens[:, at(rows[k] * BLK, BLK)]
            block = blocks[p * count + k].reshape(BLK, BLK)
            here = at(cols[k] * BLK, BLK)
            out[p, :, here] += jnp.dot(source, block, preferred_element_type=F32)
            return carry

        lax.fori_loop(0, count, step, 0, unroll=True)


def final_kernel(nf, idx, gate_rows, gate_cols, up_rows, up_cols, tokens, grad, sparse, *refs):
    pieces, hidden, grads = refs[:nf], refs[nf], refs[nf + 1]
    pre, dpre, sems = refs[nf + 2 :]
    f = idx[3]
    pairs = [(pieces[k], pre.at[(f ^ k) % 2, (f ^ k) // 2]) for k in range(nf)]
    for copy in run_copies(pairs, sems):
        copy.wait()
    width = pre.shape[3]
    for j in range(pre.shape[1]):
        here = pl.ds(j * width, width)
        gate = pre[0, j].astype(F32) + sparse[0, :, here]
        up = pre[1, j].astype(F32) + sparse[1, :, here]
        sigma = jax.nn.sigmoid(gate)
        silu = gate * sigma
        upstream = grad[:, here].astype(F32)
        dpre[0, :, here] = (upstream * up * sigma * (1.0 + gate * (1.0 - sigma))).astype(BF16)
        dpre[1, :, here] = (upstream * silu).astype(BF16)
        hidden[:, here] = (silu * up).astype(BF16)
    count = gate_rows.shape[0]
    for p, (rows, cols) in enumerate(((gate_rows, gate_cols), (up_rows, up_cols))):

        def step(k, carry, p=p, rows=rows, cols=cols):
            source = tokens[:, at(rows[k] * BLK, BLK)]
            picked = dpre[p, :, at(cols[k] * BLK, BLK)]
            value = lax.dot_general(
                source, picked, (((0,), (0,)), ((), ())), preferred_element_type=F32
            )
            grads[:, p * count + k] = value.astype(BF16).reshape(nf, BLK // nf, BLK)
            return carry

        lax.fori_loop(0, count, step, 0, unroll=True)


def exchange_device(
    mesh,
    tokens,
    gate_left,
    gate_right,
    gate_values,
    gate_rows,
    gate_cols,
    up_left,
    up_right,
    up_values,
    up_rows,
    up_cols,
    grad_hidden,
):
    nf, nt = mesh.shape["fsdp"], mesh.shape["tp"]
    nz = nf // 2
    rows, width = tokens.shape[0], gate_right.shape[1]
    depth, slice_width = gate_left.shape
    cols = width // nz
    count = gate_values.shape[0]
    share = BLK // nf
    f, t = lax.axis_index("fsdp"), lax.axis_index("tp")
    z, x, c = f // 2, f % 2, t % 2
    idx = jnp.stack([z, x, c, f, t]).astype(jnp.int32)

    def move(value, df=0, dt=0):
        pairs = [(i * nt + j, (i ^ df) * nt + (j ^ dt)) for i in range(nf) for j in range(nt)]
        return lax.ppermute(value, ("fsdp", "tp"), pairs)

    halves = [
        lax.dynamic_slice(tokens, (0, (z ^ j) * 2 * depth + c * depth), (rows, depth))
        for j in range(1, nz)
    ]
    mine = [move(h, df=2 * j) for j, h in enumerate(halves, 1)]
    recv_g, recv_u = move(gate_left, df=1), move(up_left, df=1)
    other = [move(h, dt=1) for h in mine]
    sums = pl.pallas_call(
        functools.partial(partial_kernel, nz),
        out_shape=[jax.ShapeDtypeStruct((rows, 2 * slice_width), F32)]
        + [jax.ShapeDtypeStruct((rows, 2 * slice_width), BF16)] * (nz - 1),
        in_specs=[SMEM] + [ANY] * (2 * nz + 3),
        out_specs=[VMEM] * nz,
        scratch_shapes=[
            pltpu.VMEM((2, depth, 2 * slice_width), BF16),
            pltpu.VMEM((nz, rows, 2 * depth), BF16),
            pltpu.SemaphoreType.DMA((2 * nz + 3,)),
        ],
        name="rank_partial",
    )(idx, tokens, *mine, *other, gate_left, up_left, recv_g, recv_u)
    total = sums[0]
    for j in range(1, nz):
        total = total + move(sums[j], df=2 * j).astype(F32)
    rank = total.astype(BF16)
    rank_gate, rank_up = rank[:, :slice_width], rank[:, slice_width:]
    rank_own = jnp.where(x == 0, rank_gate, rank_up)
    rank_other = jnp.where(x == 0, rank_up, rank_gate)
    slots = [rank_own] + [move(rank_other if k % 2 else rank_own, df=k) for k in range(1, nf)]
    stack = jnp.stack(slots)
    ranks = [stack, move(stack, dt=1)]
    ranks.append(move(stack, dt=2))
    ranks.append(move(ranks[2], dt=1))

    rights = []
    for k in range(nf):
        start = (0, (z ^ (k // 2)) * cols)
        size = (gate_right.shape[0], cols)
        rights.append(
            jnp.where(
                (x ^ (k % 2)) == 0,
                lax.dynamic_slice(gate_right, start, size),
                lax.dynamic_slice(up_right, start, size),
            )
        )
    rights = [rights[0]] + [move(rights[k], df=k) for k in range(1, nf)]

    own_values = jnp.concatenate([gate_values, up_values], 0).reshape(2 * count, share, BLK)
    over_z = [own_values] + [move(own_values, df=2 * j) for j in range(1, nz)]
    values = []
    for j in range(nz):
        values += [over_z[j], move(over_z[j], df=1)]
    base = t * (width // BLK)
    index = (idx, gate_rows, gate_cols - base, up_rows, up_cols - base)
    sparse = pl.pallas_call(
        functools.partial(sparse_kernel, nf),
        out_shape=jax.ShapeDtypeStruct((2, rows, width), F32),
        in_specs=[SMEM] * 5 + [VMEM] + [ANY] * nf,
        out_specs=VMEM,
        scratch_shapes=[
            pltpu.VMEM((2 * count, nf, share, BLK), BF16),
            pltpu.SemaphoreType.DMA((nf,)),
        ],
        name="sparse_forward",
    )(*index, tokens, *values)

    lowrank = pl.pallas_call(
        functools.partial(lowrank_kernel, nf, nt),
        out_shape=[jax.ShapeDtypeStruct((rows, cols), BF16)] * nf,
        in_specs=[SMEM] + [ANY] * (nt + nf),
        out_specs=[VMEM] * nf,
        scratch_shapes=[
            pltpu.VMEM((nt, nf, rows, slice_width), BF16),
            pltpu.VMEM((nf, gate_right.shape[0], cols), BF16),
            pltpu.SemaphoreType.DMA((nt + nf,)),
        ],
        name="lowrank",
    )(idx, *ranks, *rights)
    pieces = [lowrank[0]] + [move(lowrank[k], df=k) for k in range(1, nf)]

    hidden, grads = pl.pallas_call(
        functools.partial(final_kernel, nf),
        out_shape=[
            jax.ShapeDtypeStruct((rows, width), BF16),
            jax.ShapeDtypeStruct((nf, 2 * count, share, BLK), BF16),
        ],
        in_specs=[SMEM] * 5 + [VMEM] * 3 + [ANY] * nf,
        out_specs=[VMEM] * 2,
        scratch_shapes=[
            pltpu.VMEM((2, nz, rows, cols), BF16),
            pltpu.VMEM((2, rows, width), BF16),
            pltpu.SemaphoreType.DMA((nf,)),
        ],
        name="hidden_and_grads",
    )(*index, tokens, grad_hidden, sparse, *pieces)
    shares = lax.all_to_all(grads, "fsdp", 0, 0, tiled=True)
    summed = jnp.sum(shares.astype(F32), axis=0).reshape(2 * count, share * BLK)
    return hidden, summed[:count], summed[count:]


def dispatch(mesh, *args):
    nf, nt = mesh.shape["fsdp"], mesh.shape["tp"]
    width = args[2].shape[1]
    direct = nf in (4, 8) and nt == 4 and width % (BLK * (nf // 2)) == 0
    if direct:
        return exchange_device(mesh, *args)
    return on_device(*args)


def solution(mesh):
    return jax.shard_map(
        functools.partial(dispatch, mesh),
        mesh=mesh,
        in_specs=(
            P("fsdp", None),
            P("fsdp", "tp"),
            P("fsdp", "tp"),
            P("tp", "fsdp"),
            P("tp"),
            P("tp"),
            P("fsdp", "tp"),
            P("fsdp", "tp"),
            P("tp", "fsdp"),
            P("tp"),
            P("tp"),
            P("fsdp", "tp"),
        ),
        out_specs=(P("fsdp", "tp"), P("tp", "fsdp"), P("tp", "fsdp")),
        check_vma=False,
    )
```

```python
import functools

import jax
import jax.numpy as jnp
from jax import lax
from jax.experimental import pallas as pl
from jax.experimental.pallas import tpu as pltpu
from jax.sharding import Mesh
from jax.sharding import PartitionSpec as P

BLK = 128


def support_forward(tokens, blocks, rows, cols_local, col_blocks):
    width = tokens.shape[1] // BLK
    sources = tokens.reshape(tokens.shape[0], width, BLK)[:, rows, :]
    parts = jnp.einsum("tkb,kbc->tkc", sources, blocks, preferred_element_type=jnp.float32)
    placed = (
        jnp.zeros((tokens.shape[0], col_blocks, BLK), jnp.float32).at[:, cols_local, :].add(parts)
    )
    return (placed.reshape(tokens.shape[0], col_blocks * BLK), sources)


def value_terms(sources_gate, dpre_gate, local_gate, sources_up, dpre_up, local_up, col_blocks):
    picked_gate = dpre_gate.reshape(dpre_gate.shape[0], col_blocks, BLK)[:, local_gate, :]
    picked_up = dpre_up.reshape(dpre_up.shape[0], col_blocks, BLK)[:, local_up, :]
    value_gate = jnp.einsum(
        "tkb,tkc->kbc", sources_gate, picked_gate, preferred_element_type=jnp.float32
    )
    value_up = jnp.einsum("tkb,tkc->kbc", sources_up, picked_up, preferred_element_type=jnp.float32)
    return (
        value_gate.reshape(value_gate.shape[0], BLK * BLK),
        value_up.reshape(value_up.shape[0], BLK * BLK),
    )


def on_device(
    tokens,
    gate_left,
    gate_right,
    gate_values,
    gate_rows,
    gate_cols,
    up_left,
    up_right,
    up_values,
    up_rows,
    up_cols,
    grad_hidden,
):
    left_gate, left_up = (
        lax.all_gather(gate_left, "fsdp", axis=0, tiled=True),
        lax.all_gather(up_left, "fsdp", axis=0, tiled=True),
    )
    rank_gate = jnp.dot(tokens, left_gate, preferred_element_type=jnp.float32).astype(jnp.bfloat16)
    rank_up = jnp.dot(tokens, left_up, preferred_element_type=jnp.float32).astype(jnp.bfloat16)
    full_gate, full_up = (
        lax.all_gather(rank_gate, "tp", axis=1, tiled=True),
        lax.all_gather(rank_up, "tp", axis=1, tiled=True),
    )
    flat_gate, flat_up = (
        lax.all_gather(gate_values, "fsdp", axis=1, tiled=True),
        lax.all_gather(up_values, "fsdp", axis=1, tiled=True),
    )
    blocks_gate = flat_gate.reshape(flat_gate.shape[0], BLK, BLK)
    blocks_up = flat_up.reshape(flat_up.shape[0], BLK, BLK)
    right_gate = lax.all_gather(gate_right, "fsdp", axis=0, tiled=True)
    right_up = lax.all_gather(up_right, "fsdp", axis=0, tiled=True)
    col_blocks = right_gate.shape[1] // BLK
    col_base = lax.axis_index("tp") * col_blocks
    local_gate = gate_cols - col_base
    local_up = up_cols - col_base
    sparse_gate, sources_gate = support_forward(
        tokens, blocks_gate, gate_rows, local_gate, col_blocks
    )
    sparse_up, sources_up = support_forward(tokens, blocks_up, up_rows, local_up, col_blocks)
    pre_gate = jnp.dot(full_gate, right_gate, preferred_element_type=jnp.float32) + sparse_gate
    pre_up = jnp.dot(full_up, right_up, preferred_element_type=jnp.float32) + sparse_up
    sigma = jax.nn.sigmoid(pre_gate)
    silu = pre_gate * sigma
    upstream = grad_hidden.astype(jnp.float32)
    dpre_gate = (upstream * pre_up * sigma * (1.0 + pre_gate * (1.0 - sigma))).astype(jnp.bfloat16)
    dpre_up = (upstream * silu).astype(jnp.bfloat16)
    hidden = (silu * pre_up).astype(jnp.bfloat16)
    value_gate, value_up = value_terms(
        sources_gate, dpre_gate, local_gate, sources_up, dpre_up, local_up, col_blocks
    )
    grad_gate_values, grad_up_values = (
        lax.psum_scatter(value_gate, "fsdp", scatter_dimension=1, tiled=True),
        lax.psum_scatter(value_up, "fsdp", scatter_dimension=1, tiled=True),
    )
    return (hidden, grad_gate_values, grad_up_values)


ANY = pl.BlockSpec(memory_space=pl.ANY)
VMEM = pl.BlockSpec(memory_space=pltpu.VMEM)
SMEM = pl.BlockSpec(memory_space=pltpu.SMEM)
BF16, F32 = jnp.bfloat16, jnp.float32
AXES = ("z", "x", "y", "c")


def at(start, size):
    return pl.ds(pl.multiple_of(start, BLK), size)


def run_copies(pairs, sems):
    copies = [pltpu.make_async_copy(s, d, sems.at[i]) for i, (s, d) in enumerate(pairs)]
    for copy in copies:
        copy.start()
    return copies


def partial_kernel(nz, idx, tokens, *refs):
    mine, other = refs[: nz - 1], refs[nz - 1 : 2 * nz - 2]
    left_g, left_u, recv_g, recv_u = refs[2 * nz - 2 : 2 * nz + 2]
    own_out, outs = refs[2 * nz + 2], refs[2 * nz + 3 : 3 * nz + 2]
    left, toks, sems = refs[3 * nz + 2 :]
    z, x, c = idx[0], idx[1], idx[2]
    depth, width = left_g.shape
    pairs = [
        (left_g, left.at[x, :, pl.ds(0, width)]),
        (left_u, left.at[x, :, pl.ds(width, width)]),
        (recv_g, left.at[1 - x, :, pl.ds(0, width)]),
        (recv_u, left.at[1 - x, :, pl.ds(width, width)]),
        (tokens.at[:, at(z * 2 * depth, 2 * depth)], toks.at[0]),
    ]
    for j in range(1, nz):
        pairs.append((mine[j - 1], toks.at[j, :, at(c * depth, depth)]))
        pairs.append((other[j - 1], toks.at[j, :, at((1 - c) * depth, depth)]))
    for copy in run_copies(pairs, sems):
        copy.wait()
    weights = left[...].reshape(2 * depth, 2 * width)
    rows = toks.shape[1]
    total = jnp.dot(
        toks[...].reshape(nz * rows, 2 * depth), weights, preferred_element_type=F32
    )
    own_out[...] = total[:rows]
    for j in range(1, nz):
        outs[j - 1][...] = total[j * rows : (j + 1) * rows].astype(BF16)


def rank_round_kernel(own, *refs):
    others, out = refs[:-1], refs[-1]
    total = own[...]
    for other in others:
        total = total + other[...].astype(F32)
    width = out.shape[2]
    for k in range(out.shape[0]):
        out[k] = total[:, k % 2 * width : (k % 2 + 1) * width].astype(BF16)


def lowrank_kernel(nf, nt, slots, idx, *refs):
    ranks, rights = refs[:nt], refs[nt : nt + nf]
    outs = refs[nt + nf : nt + nf + len(slots)]
    rank, weight, sems = refs[nt + nf + len(slots) :]
    f, t = idx[3], idx[4]
    slice_width = ranks[0].shape[2]
    pairs = [(rights[k], weight.at[f ^ k]) for k in range(nf)]
    for s in range(nt):
        lanes = at((t ^ s) * slice_width, slice_width)
        pairs += [(ranks[s].at[f ^ m], rank.at[i, :, lanes]) for i, m in enumerate(slots)]
    for copy in run_copies(pairs, sems):
        copy.wait()
    count, rows, depth = rank.shape
    cols = weight.shape[2]
    weights = weight[...].reshape(depth, cols)
    total = jnp.dot(rank[...].reshape(count * rows, depth), weights, preferred_element_type=F32)
    for i in range(count):
        outs[i][...] = total[i * rows : (i + 1) * rows].astype(BF16)


def sparse_kernel(nf, idx, gate_rows, gate_cols, up_rows, up_cols, tokens, *refs):
    values, out, blocks, sems = refs[:nf], refs[nf], refs[nf + 1], refs[nf + 2]
    z, f = idx[0], idx[3]
    inner = jnp.logical_or(z == 1, z == 2)
    across = jnp.where(inner, 6, 4)
    slots = [0, 1, 2, 3, across, across + 1, 10 - across, 11 - across]
    copies = run_copies([(v, blocks.at[:, f ^ k]) for v, k in zip(values, slots)], sems)
    out[...] = jnp.zeros_like(out)
    for copy in copies:
        copy.wait()
    count = gate_rows.shape[0]
    for p, (rows, cols) in enumerate(((gate_rows, gate_cols), (up_rows, up_cols))):

        def step(k, carry, p=p, rows=rows, cols=cols):
            source = tokens[:, at(rows[k] * BLK, BLK)]
            block = blocks[p * count + k].reshape(BLK, BLK)
            here = at(cols[k] * BLK, BLK)
            out[p, :, here] += jnp.dot(source, block, preferred_element_type=F32)
            return carry

        lax.fori_loop(0, count, step, 0, unroll=True)


def final_kernel(nf, idx, gate_rows, gate_cols, up_rows, up_cols, *refs):
    nz = nf // 2
    tokens_in, grad_in, sparse_in = refs[:3]
    pieces = refs[3 : nf + 3]
    hidden_out, gate_keep_out, gate_send_out, up_keep_out = refs[nf + 3 : nf + 7]
    up_send_outs = refs[nf + 7 : nf + 6 + nz]
    tokens, grad, sparse, pre, dpre, hidden = refs[nf + 6 + nz : nf + 12 + nz]
    gate_keep, gate_send, up_keep, up_send, sems, out_sems = refs[nf + 12 + nz :]
    z, x, f = idx[0], idx[1], idx[3]
    width = pre.shape[3]
    pairs = [(pieces[k], pre.at[(f ^ k) % 2, (f ^ k) // 2]) for k in range(nf)]
    for j in range(nz):
        here = pl.ds(j * width, width)
        pairs.append((sparse_in.at[:, :, here], sparse.at[:, :, here]))
        pairs.append((grad_in.at[:, here], grad.at[:, here]))
    pairs.append((tokens_in, tokens))
    copies = run_copies(pairs, sems)
    for copy in copies[:nf]:
        copy.wait()
    sent = []

    def send(source, target):
        copy = pltpu.make_async_copy(source, target, out_sems.at[len(sent)])
        copy.start()
        sent.append(copy)

    for j in range(nz):
        here = pl.ds(j * width, width)
        copies[nf + 2 * j].wait()
        copies[nf + 2 * j + 1].wait()
        gate = pre[0, j].astype(F32) + sparse[0, :, here]
        up = pre[1, j].astype(F32) + sparse[1, :, here]
        sigma = jax.nn.sigmoid(gate)
        silu = gate * sigma
        upstream = grad[:, here].astype(F32)
        dpre[0, :, here] = (upstream * up * sigma * (1.0 + gate * (1.0 - sigma))).astype(BF16)
        dpre[1, :, here] = (upstream * silu).astype(BF16)
        hidden[:, here] = (silu * up).astype(BF16)
        send(hidden.at[:, here], hidden_out.at[:, here])
    copies[-1].wait()
    count = gate_rows.shape[0]

    def partial(p, rows, cols, k):
        source = tokens[:, at(rows[k] * BLK, BLK)]
        picked = dpre[p, :, at(cols[k] * BLK, BLK)]
        value = lax.dot_general(
            source, picked, (((0,), (0,)), ((), ())), preferred_element_type=F32
        )
        return value.reshape(nz, 2, BLK // nf, BLK)

    def up_step(k, carry):
        value = partial(1, up_rows, up_cols, k)
        for j in range(nz):
            up_keep[z ^ j, :, k] = value[j]
            up_send[z ^ j, :, k] = value[j].astype(BF16)
        return carry

    def gate_step(k, carry):
        value = partial(0, gate_rows, gate_cols, k)
        keep = jnp.where(x == 0, value[:, 0], value[:, 1])
        other = jnp.where(x == 0, value[:, 1], value[:, 0]).astype(BF16)
        for j in range(nz):
            gate_keep[z ^ j, k] = keep[j]
            gate_send[z ^ j, k] = other[j]
        return carry

    lax.fori_loop(0, count, up_step, 0, unroll=True)
    for j in range(1, nz):
        send(up_send.at[j], up_send_outs[j - 1])
    send(up_keep.at[0], up_keep_out)
    lax.fori_loop(0, count, gate_step, 0, unroll=True)
    send(gate_send, gate_send_out)
    send(gate_keep, gate_keep_out)
    for copy in sent:
        copy.wait()


def gate_add_kernel(keep, got, own, *sends):
    own[...] = keep[0] + got[0].astype(F32)
    for j, send in enumerate(sends, 1):
        send[...] = (keep[j] + got[j].astype(F32)).astype(BF16)


def exchange_device(
    mesh,
    tokens,
    gate_left,
    gate_right,
    gate_values,
    gate_rows,
    gate_cols,
    up_left,
    up_right,
    up_values,
    up_rows,
    up_cols,
    grad_hidden,
):
    nf, nt = mesh.shape["fsdp"], mesh.shape["tp"]
    nz = nf // 2
    rows, width = tokens.shape[0], gate_right.shape[1]
    depth, slice_width = gate_left.shape
    cols = width // nz
    count = gate_values.shape[0]
    share = BLK // nf
    z, x, c = lax.axis_index("z"), lax.axis_index("x"), lax.axis_index("c")
    f, t = 2 * z + x, 2 * lax.axis_index("y") + c
    idx = jnp.stack([z, x, c, f, t]).astype(jnp.int32)

    def move(value, df=0, dt=0, only=range(nf)):
        pairs = [(i, i ^ (df * nt + dt)) for i in range(nf * nt) if i // (2 * nt) in only]
        return lax.ppermute(value, AXES, pairs)

    halves = [
        lax.dynamic_slice(tokens, (0, (z ^ j) * 2 * depth + c * depth), (rows, depth))
        for j in range(1, nz)
    ]
    mine = [move(h, df=2 * j) for j, h in enumerate(halves, 1)]
    recv_g, recv_u = move(gate_left, df=1), move(up_left, df=1)
    other = [move(h, dt=1) for h in mine]
    sums = pl.pallas_call(
        functools.partial(partial_kernel, nz),
        out_shape=[jax.ShapeDtypeStruct((rows, 2 * slice_width), F32)]
        + [jax.ShapeDtypeStruct((rows, 2 * slice_width), BF16)] * (nz - 1),
        in_specs=[SMEM] + [ANY] * (2 * nz + 3),
        out_specs=[VMEM] * nz,
        scratch_shapes=[
            pltpu.VMEM((2, depth, 2 * slice_width), BF16),
            pltpu.VMEM((nz, rows, 2 * depth), BF16),
            pltpu.SemaphoreType.DMA((2 * nz + 3,)),
        ],
        name="rank_partial",
    )(idx, tokens, *mine, *other, gate_left, up_left, recv_g, recv_u)
    got = [move(sums[j], df=2 * j) for j in range(1, nz)]
    for_f = pl.pallas_call(
        rank_round_kernel,
        out_shape=jax.ShapeDtypeStruct((nf, rows, slice_width), BF16),
        in_specs=[VMEM] * nz,
        out_specs=VMEM,
        name="rank_round",
    )(sums[0], *got)
    stack = lax.all_to_all(for_f, ("z", "x"), 0, 0, tiled=True)
    ranks = [stack, move(stack, dt=1), move(stack, dt=2)]
    ranks.append(move(ranks[2], dt=1))

    rights = []
    for k in range(nf):
        start = (0, (z ^ (k // 2)) * cols)
        size = (gate_right.shape[0], cols)
        rights.append(
            jnp.where(
                (x ^ (k % 2)) == 0,
                lax.dynamic_slice(gate_right, start, size),
                lax.dynamic_slice(up_right, start, size),
            )
        )
    rights = [rights[0]] + [move(rights[k], df=k) for k in range(1, nf)]

    own_values = jnp.concatenate([gate_values, up_values], 0).reshape(2 * count, share, BLK)
    near = move(own_values, df=2)
    inner = (z == 1) | (z == 2)
    from_across = [
        jnp.where(inner, got, move(got, df=2, only=(1, 2)))
        for got in (move(v, df=6, only=(1, 2)) for v in (own_values, near))
    ]
    values = [own_values, move(own_values, df=1)]
    values += [near, move(near, df=1)]
    for v in from_across:
        values += [v, move(v, df=1)]
    base = t * (width // BLK)
    index = (idx, gate_rows, gate_cols - base, up_rows, up_cols - base)
    sparse = pl.pallas_call(
        functools.partial(sparse_kernel, nf),
        out_shape=jax.ShapeDtypeStruct((2, rows, width), F32),
        in_specs=[SMEM] * 5 + [VMEM] + [ANY] * nf,
        out_specs=VMEM,
        scratch_shapes=[
            pltpu.VMEM((2 * count, nf, share, BLK), BF16),
            pltpu.SemaphoreType.DMA((nf,)),
        ],
        name="sparse_forward",
    )(*index, tokens, *values)

    pieces = [None] * nf
    for slots in (range(nf // 2, nf), range(nf // 2)):
        lowrank = pl.pallas_call(
            functools.partial(lowrank_kernel, nf, nt, slots),
            out_shape=[jax.ShapeDtypeStruct((rows, cols), BF16)] * len(slots),
            in_specs=[SMEM] + [ANY] * (nt + nf),
            out_specs=[VMEM] * len(slots),
            scratch_shapes=[
                pltpu.VMEM((len(slots), rows, nt * slice_width), BF16),
                pltpu.VMEM((nf, gate_right.shape[0], cols), BF16),
                pltpu.SemaphoreType.DMA((nt * len(slots) + nf,)),
            ],
            name="lowrank",
        )(idx, *ranks, *rights)
        for k, product in zip(slots, lowrank):
            pieces[k] = move(product, df=k) if k else product

    support = (count, share, BLK)
    outs = pl.pallas_call(
        functools.partial(final_kernel, nf),
        out_shape=[
            jax.ShapeDtypeStruct((rows, width), BF16),
            jax.ShapeDtypeStruct((nz,) + support, F32),
            jax.ShapeDtypeStruct((nz,) + support, BF16),
            jax.ShapeDtypeStruct((2,) + support, F32),
        ]
        + [jax.ShapeDtypeStruct((2,) + support, BF16)] * (nz - 1),
        in_specs=[SMEM] * 5 + [ANY] * (nf + 3),
        out_specs=[ANY] * (nz + 3),
        scratch_shapes=[
            pltpu.VMEM(tokens.shape, BF16),
            pltpu.VMEM((rows, width), BF16),
            pltpu.VMEM((2, rows, width), F32),
            pltpu.VMEM((2, nz, rows, cols), BF16),
            pltpu.VMEM((2, rows, width), BF16),
            pltpu.VMEM((rows, width), BF16),
            pltpu.VMEM((nz,) + support, F32),
            pltpu.VMEM((nz,) + support, BF16),
            pltpu.VMEM((nz, 2) + support, F32),
            pltpu.VMEM((nz, 2) + support, BF16),
            pltpu.SemaphoreType.DMA((nf + 2 * nz + 1,)),
            pltpu.SemaphoreType.DMA((2 * nz + 2,)),
        ],
        name="hidden_and_grads",
    )(*index, tokens, grad_hidden, sparse, *pieces)
    hidden, gate_keep, gate_send, up_keep, *up_sends = outs

    up_sum = up_keep
    for j in range(1, nz):
        up_sum = up_sum + move(up_sends[j - 1], df=2 * j).astype(F32)
    gate_got = move(gate_send, df=1)
    gate_total, *gate_sums = pl.pallas_call(
        gate_add_kernel,
        out_shape=[jax.ShapeDtypeStruct(support, F32)]
        + [jax.ShapeDtypeStruct(support, BF16)] * (nz - 1),
        in_specs=[VMEM] * 2,
        out_specs=[VMEM] * nz,
        name="gate_add",
    )(gate_keep, gate_got)
    for j in range(1, nz):
        gate_total = gate_total + move(gate_sums[j - 1], df=2 * j).astype(F32)
    up_here = jnp.where(x == 0, up_sum[0], up_sum[1])
    up_there = jnp.where(x == 0, up_sum[1], up_sum[0]).astype(BF16)
    up_total = up_here + move(up_there, df=1).astype(F32)
    return hidden, gate_total.reshape(count, share * BLK), up_total.reshape(count, share * BLK)


def placed(mesh, axes, step):
    fsdp, tp = axes
    both = P(fsdp, tp)
    swapped = P(tp, fsdp)
    return jax.shard_map(
        step,
        mesh=mesh,
        in_specs=(P(fsdp, None),) + (both, both, swapped, P(tp), P(tp)) * 2 + (both,),
        out_specs=(both, swapped, swapped),
        check_vma=False,
    )


def solution(mesh):
    nf, nt = mesh.shape["fsdp"], mesh.shape["tp"]

    def step(*args):
        width = args[2].shape[1] // nt
        if nf == 8 and nt == 4 and width % (BLK * (nf // 2)) == 0:
            split = Mesh(mesh.devices.reshape(nf // 2, 2, 2, 2), AXES)

            def body(*local):
                return exchange_device(mesh, *local)

            return placed(split, (("z", "x"), ("y", "c")), body)(*args)
        return placed(mesh, ("fsdp", "tp"), on_device)(*args)

    return step
```

```python
import functools

import jax
import jax.numpy as jnp
from jax import lax
from jax.experimental import pallas as pl
from jax.experimental.pallas import tpu as pltpu
from jax.sharding import Mesh
from jax.sharding import PartitionSpec as P

BLK = 128


def support_forward(tokens, blocks, rows, cols_local, col_blocks):
    width = tokens.shape[1] // BLK
    sources = tokens.reshape(tokens.shape[0], width, BLK)[:, rows, :]
    parts = jnp.einsum("tkb,kbc->tkc", sources, blocks, preferred_element_type=jnp.float32)
    placed = (
        jnp.zeros((tokens.shape[0], col_blocks, BLK), jnp.float32).at[:, cols_local, :].add(parts)
    )
    return (placed.reshape(tokens.shape[0], col_blocks * BLK), sources)


def value_terms(sources_gate, dpre_gate, local_gate, sources_up, dpre_up, local_up, col_blocks):
    picked_gate = dpre_gate.reshape(dpre_gate.shape[0], col_blocks, BLK)[:, local_gate, :]
    picked_up = dpre_up.reshape(dpre_up.shape[0], col_blocks, BLK)[:, local_up, :]
    value_gate = jnp.einsum(
        "tkb,tkc->kbc", sources_gate, picked_gate, preferred_element_type=jnp.float32
    )
    value_up = jnp.einsum("tkb,tkc->kbc", sources_up, picked_up, preferred_element_type=jnp.float32)
    return (
        value_gate.reshape(value_gate.shape[0], BLK * BLK),
        value_up.reshape(value_up.shape[0], BLK * BLK),
    )


def on_device(
    tokens,
    gate_left,
    gate_right,
    gate_values,
    gate_rows,
    gate_cols,
    up_left,
    up_right,
    up_values,
    up_rows,
    up_cols,
    grad_hidden,
):
    left_gate, left_up = (
        lax.all_gather(gate_left, "fsdp", axis=0, tiled=True),
        lax.all_gather(up_left, "fsdp", axis=0, tiled=True),
    )
    rank_gate = jnp.dot(tokens, left_gate, preferred_element_type=jnp.float32).astype(jnp.bfloat16)
    rank_up = jnp.dot(tokens, left_up, preferred_element_type=jnp.float32).astype(jnp.bfloat16)
    full_gate, full_up = (
        lax.all_gather(rank_gate, "tp", axis=1, tiled=True),
        lax.all_gather(rank_up, "tp", axis=1, tiled=True),
    )
    flat_gate, flat_up = (
        lax.all_gather(gate_values, "fsdp", axis=1, tiled=True),
        lax.all_gather(up_values, "fsdp", axis=1, tiled=True),
    )
    blocks_gate = flat_gate.reshape(flat_gate.shape[0], BLK, BLK)
    blocks_up = flat_up.reshape(flat_up.shape[0], BLK, BLK)
    right_gate = lax.all_gather(gate_right, "fsdp", axis=0, tiled=True)
    right_up = lax.all_gather(up_right, "fsdp", axis=0, tiled=True)
    col_blocks = right_gate.shape[1] // BLK
    col_base = lax.axis_index("tp") * col_blocks
    local_gate = gate_cols - col_base
    local_up = up_cols - col_base
    sparse_gate, sources_gate = support_forward(
        tokens, blocks_gate, gate_rows, local_gate, col_blocks
    )
    sparse_up, sources_up = support_forward(tokens, blocks_up, up_rows, local_up, col_blocks)
    pre_gate = jnp.dot(full_gate, right_gate, preferred_element_type=jnp.float32) + sparse_gate
    pre_up = jnp.dot(full_up, right_up, preferred_element_type=jnp.float32) + sparse_up
    sigma = jax.nn.sigmoid(pre_gate)
    silu = pre_gate * sigma
    upstream = grad_hidden.astype(jnp.float32)
    dpre_gate = (upstream * pre_up * sigma * (1.0 + pre_gate * (1.0 - sigma))).astype(jnp.bfloat16)
    dpre_up = (upstream * silu).astype(jnp.bfloat16)
    hidden = (silu * pre_up).astype(jnp.bfloat16)
    value_gate, value_up = value_terms(
        sources_gate, dpre_gate, local_gate, sources_up, dpre_up, local_up, col_blocks
    )
    grad_gate_values, grad_up_values = (
        lax.psum_scatter(value_gate, "fsdp", scatter_dimension=1, tiled=True),
        lax.psum_scatter(value_up, "fsdp", scatter_dimension=1, tiled=True),
    )
    return (hidden, grad_gate_values, grad_up_values)


ANY = pl.BlockSpec(memory_space=pl.ANY)
VMEM = pl.BlockSpec(memory_space=pltpu.VMEM)
SMEM = pl.BlockSpec(memory_space=pltpu.SMEM)
BF16, F32 = jnp.bfloat16, jnp.float32
AXES = ("z", "x", "y", "c")


def grant(mib):
    return pltpu.CompilerParams(vmem_limit_bytes=mib << 20)


def at(start, size):
    return pl.ds(pl.multiple_of(start, BLK), size)


def run_copies(pairs, sems):
    copies = [pltpu.make_async_copy(s, d, sems.at[i]) for i, (s, d) in enumerate(pairs)]
    for copy in copies:
        copy.start()
    return copies


def partial_kernel(nz, idx, tokens, *refs):
    n = nz - 1
    quarters, (left_g, left_u, recv_g, recv_u) = refs[: 4 * n], refs[4 * n : 4 * nz]
    own_out, outs = refs[4 * nz], refs[4 * nz + 1 : 5 * nz]
    left, toks = refs[5 * nz :]
    z, x, c, y = idx[0], idx[1], idx[2], idx[5]
    depth, width = left_g.shape
    left[x, :, :width], left[x, :, width:] = left_g[...], left_u[...]
    left[1 - x, :, :width], left[1 - x, :, width:] = recv_g[...], recv_u[...]
    toks[0] = tokens[:, at(z * 2 * depth, 2 * depth)]
    quarter = depth // 2
    for i, (dc, dy) in enumerate(((0, 0), (0, 1), (1, 0), (1, 1))):
        start = (c ^ dc) * depth + (y ^ dy) * quarter
        for j in range(1, nz):
            toks[j, :, at(start, quarter)] = quarters[i * n + j - 1][...]
    weights = left[...].reshape(2 * depth, 2 * width)
    rows = toks.shape[1]
    total = jnp.dot(
        toks[...].reshape(nz * rows, 2 * depth), weights, preferred_element_type=F32
    )
    own_out[...] = total[:rows]
    for j in range(1, nz):
        outs[j - 1][...] = total[j * rows : (j + 1) * rows].astype(BF16)


def rank_round_kernel(own, *refs):
    others, out = refs[:-1], refs[-1]
    total = own[...]
    for other in others:
        total = total + other[...].astype(F32)
    width = out.shape[2]
    for k in range(out.shape[0]):
        out[k] = total[:, k % 2 * width : (k % 2 + 1) * width].astype(BF16)


def load_ranks(nf, slots, idx, ranks, rank):
    f, t = idx[3], idx[4]
    depth = rank.shape[2] // nf
    parts = ranks[0].shape[2] // depth
    for s, source in enumerate(ranks):
        for h in range(parts):
            lanes = at((f ^ ((t ^ s) * parts + h)) * depth, depth)
            for i, m in enumerate(slots):
                rank[i, :, lanes] = source[f ^ m, :, h * depth : (h + 1) * depth]


def product(rank, rights):
    count, rows, _ = rank.shape
    weights = jnp.concatenate([right[...] for right in rights], axis=0)
    lhs = rank[:, :, : weights.shape[0]].reshape(count * rows, weights.shape[0])
    return jnp.dot(lhs, weights, preferred_element_type=F32)


def lowrank_kernel(nf, nt, slots, idx, *refs):
    ranks, rights = refs[:nt], refs[nt : nt + nf]
    outs, rank = refs[nt + nf : nt + nf + len(slots)], refs[-1]
    load_ranks(nf, slots, idx, ranks, rank)
    total = product(rank, rights)
    rows = rank.shape[1]
    for i in range(len(slots)):
        outs[i][...] = total[i * rows : (i + 1) * rows].astype(BF16)


def lowrank_first_kernel(nf, nt, slots, idx, *refs):
    ranks, rights = refs[:nt], refs[nt : nt + nf - 1]
    total, columns, rank = refs[nt + nf - 1 :]
    load_ranks(nf, slots, idx, ranks, rank)
    total[...] = product(rank, rights)
    columns[...] = rank[:, :, -columns.shape[1] :].reshape(columns.shape)


def lowrank_last_kernel(total, columns, right, *outs):
    rows = outs[0].shape[0]
    value = total[...] + jnp.dot(columns[...], right[...], preferred_element_type=F32)
    for i, out in enumerate(outs):
        out[...] = value[i * rows : (i + 1) * rows].astype(BF16)


def sparse_kernel(nf, idx, gate_rows, gate_cols, up_rows, up_cols, tokens, *refs):
    values, out, blocks, sems = refs[:nf], refs[nf], refs[nf + 1], refs[nf + 2]
    z, f = idx[0], idx[3]
    inner = jnp.logical_or(z == 1, z == 2)
    across = jnp.where(inner, 6, 4)
    slots = [0, 1, 2, 3, across, across + 1, 10 - across, 11 - across]
    copies = run_copies([(v, blocks.at[:, f ^ k]) for v, k in zip(values, slots)], sems)
    out[...] = jnp.zeros_like(out)
    for copy in copies:
        copy.wait()
    count = gate_rows.shape[0]
    for p, (rows, cols) in enumerate(((gate_rows, gate_cols), (up_rows, up_cols))):

        def step(k, carry, p=p, rows=rows, cols=cols):
            source = tokens[:, at(rows[k] * BLK, BLK)]
            block = blocks[p * count + k].reshape(BLK, BLK)
            here = at(cols[k] * BLK, BLK)
            out[p, :, here] += jnp.dot(source, block, preferred_element_type=F32)
            return carry

        lax.fori_loop(0, count, step, 0, unroll=True)


def support_grads(nf, tokens, dpre, rows, cols, k):
    source = tokens[:, at(rows[k] * BLK, BLK)]
    picked = dpre[:, at(cols[k] * BLK, BLK)]
    value = lax.dot_general(source, picked, (((0,), (0,)), ((), ())), preferred_element_type=F32)
    return value.reshape(nf // 2, 2, BLK // nf, BLK)


def final_kernel(nf, idx, up_rows, up_cols, tokens, grad, sparse, *refs):
    nz = nf // 2
    pieces = refs[:nf]
    hidden, dpre_gate, up_keep = refs[nf : nf + 3]
    up_sends = refs[nf + 3 : nf + 2 + nz]
    dpre_up, keep, send = refs[nf + 2 + nz :]
    z, x = idx[0], idx[1]
    rows, width = pieces[0].shape
    tall = rows // 2
    for j in range(nz):
        mine, other = pieces[2 * j], pieces[2 * j + 1]

        def chunk(i, carry, j=j, mine=mine, other=other):
            down = pl.ds(pl.multiple_of(i % 2 * tall, tall), tall)
            local = at(i // 2 * BLK, BLK)
            here = at((z ^ j) * width + i // 2 * BLK, BLK)
            a, b = mine[down, local].astype(F32), other[down, local].astype(F32)
            gate = jnp.where(x == 0, a, b) + sparse[0, down, here]
            up = jnp.where(x == 0, b, a) + sparse[1, down, here]
            sigma = jax.nn.sigmoid(gate)
            silu = gate * sigma
            upstream = grad[down, here].astype(F32)
            slope = upstream * up * sigma * (1.0 + gate * (1.0 - sigma))
            dpre_gate[down, here] = slope.astype(BF16)
            dpre_up[down, here] = (upstream * silu).astype(BF16)
            hidden[down, here] = (silu * up).astype(BF16)
            return carry

        lax.fori_loop(0, 2 * width // BLK, chunk, 0, unroll=True)

    def step(k, carry):
        value = support_grads(nf, tokens, dpre_up, up_rows, up_cols, k)
        for j in range(nz):
            keep[z ^ j, :, k] = value[j]
            send[z ^ j, :, k] = value[j].astype(BF16)
        return carry

    lax.fori_loop(0, up_rows.shape[0], step, 0, unroll=True)
    up_keep[...] = keep[0]
    for j in range(1, nz):
        up_sends[j - 1][...] = send[j]


def gate_grads_kernel(nf, idx, rows, cols, tokens, dpre, keep_out, send_out):
    z, x = idx[0], idx[1]

    def step(k, carry):
        value = support_grads(nf, tokens, dpre, rows, cols, k)
        keep = jnp.where(x == 0, value[:, 0], value[:, 1])
        other = jnp.where(x == 0, value[:, 1], value[:, 0]).astype(BF16)
        for j in range(nf // 2):
            keep_out[z ^ j, k] = keep[j]
            send_out[z ^ j, k] = other[j]
        return carry

    lax.fori_loop(0, rows.shape[0], step, 0, unroll=True)


def gate_add_kernel(keep, got, own, *sends):
    own[...] = keep[0] + got[0].astype(F32)
    for j, send in enumerate(sends, 1):
        send[...] = (keep[j] + got[j].astype(F32)).astype(BF16)


def exchange_device(
    mesh,
    tokens,
    gate_left,
    gate_right,
    gate_values,
    gate_rows,
    gate_cols,
    up_left,
    up_right,
    up_values,
    up_rows,
    up_cols,
    grad_hidden,
):
    nf, nt = mesh.shape["fsdp"], mesh.shape["tp"]
    nz = nf // 2
    rows, width = tokens.shape[0], gate_right.shape[1]
    depth, slice_width = gate_left.shape
    cols = width // nz
    count = gate_values.shape[0]
    share = BLK // nf
    z, x, c = lax.axis_index("z"), lax.axis_index("x"), lax.axis_index("c")
    y = lax.axis_index("y")
    f, t = 2 * z + x, 2 * y + c
    idx = jnp.stack([z, x, c, f, t, y]).astype(jnp.int32)

    def move(value, df=0, dt=0, only=range(nf)):
        pairs = [(i, i ^ (df * nt + dt)) for i in range(nf * nt) if i // (2 * nt) in only]
        return lax.ppermute(value, AXES, pairs)

    quarter = depth // 2
    fetched = [
        lax.dynamic_slice(
            tokens, (0, (z ^ j) * 2 * depth + c * depth + y * quarter), (rows, quarter)
        )
        for j in range(1, nz)
    ]
    fetched = [move(part, df=2 * j) for j, part in enumerate(fetched, 1)]
    recv_g, recv_u = move(gate_left, df=1), move(up_left, df=1)
    across_y = [move(part, dt=2) for part in fetched]
    half = [*fetched, *across_y]
    half += [move(part, dt=1) for part in half]
    sums = pl.pallas_call(
        functools.partial(partial_kernel, nz),
        out_shape=[jax.ShapeDtypeStruct((rows, 2 * slice_width), F32)]
        + [jax.ShapeDtypeStruct((rows, 2 * slice_width), BF16)] * (nz - 1),
        in_specs=[SMEM] + [VMEM] * (4 * nz + 1),
        out_specs=[VMEM] * nz,
        scratch_shapes=[
            pltpu.VMEM((2, depth, 2 * slice_width), BF16),
            pltpu.VMEM((nz, rows, 2 * depth), BF16),
        ],
        name="rank_partial",
            compiler_params=grant(10),
    )(idx, tokens, *half, gate_left, up_left, recv_g, recv_u)
    got = [move(sums[j], df=2 * j) for j in range(1, nz)]
    for_f = pl.pallas_call(
        rank_round_kernel,
        out_shape=jax.ShapeDtypeStruct((nf, rows, slice_width), BF16),
        in_specs=[VMEM] * nz,
        out_specs=VMEM,
        name="rank_round",
        compiler_params=grant(4),
    )(sums[0], *got)
    stack = lax.all_to_all(for_f, ("z", "x"), 0, 0, tiled=True)
    ranks = [stack, move(stack, dt=1), move(stack, dt=2)]
    ranks.append(move(ranks[2], dt=1))

    rights = []
    later_gate, later_up, _ = lax.optimization_barrier((gate_right, up_right, fetched[0]))
    for k in range(nf):
        gate_k, up_k = (gate_right, up_right) if k in (4, 5) else (later_gate, later_up)
        start = (0, (z ^ (k // 2)) * cols)
        size = (gate_right.shape[0], cols)
        rights.append(
            jnp.where(
                (x ^ (k % 2)) == 0,
                lax.dynamic_slice(gate_k, start, size),
                lax.dynamic_slice(up_k, start, size),
            )
        )
    rights = [rights[0]] + [move(rights[k], df=k) for k in range(1, nf)]

    own_values = jnp.concatenate([gate_values, up_values], 0).reshape(2 * count, share, BLK)
    near = move(own_values, df=2)
    inner = (z == 1) | (z == 2)
    from_across = [
        jnp.where(inner, got, move(got, df=2, only=(1, 2)))
        for got in (move(v, df=6, only=(1, 2)) for v in (own_values, near))
    ]
    values = [own_values, move(own_values, df=1)]
    values += [near, move(near, df=1)]
    for v in from_across:
        values += [v, move(v, df=1)]
    base = t * (width // BLK)
    index = (idx, gate_rows, gate_cols - base, up_rows, up_cols - base)
    sparse = pl.pallas_call(
        functools.partial(sparse_kernel, nf),
        out_shape=jax.ShapeDtypeStruct((2, rows, width), F32),
        in_specs=[SMEM] * 5 + [VMEM] + [ANY] * nf,
        out_specs=VMEM,
        scratch_shapes=[
            pltpu.VMEM((2 * count, nf, share, BLK), BF16),
            pltpu.SemaphoreType.DMA((nf,)),
        ],
        name="sparse_forward",
        compiler_params=grant(14),
    )(*index, tokens, *values)

    depth_k, far, near_slots = gate_right.shape[0], range(nf // 2, nf), range(nf // 2)
    scratch = [pltpu.VMEM((nf // 2, rows, nt * slice_width), BF16)]
    blocks = [jax.ShapeDtypeStruct((rows, cols), BF16)] * (nf // 2)
    first, columns = pl.pallas_call(
        functools.partial(lowrank_first_kernel, nf, nt, far),
        out_shape=[
            jax.ShapeDtypeStruct((nf // 2 * rows, cols), F32),
            jax.ShapeDtypeStruct((nf // 2 * rows, depth_k), BF16),
        ],
        in_specs=[SMEM] + [VMEM] * (nt + nf - 1),
        out_specs=[VMEM] * 2,
        scratch_shapes=scratch,
        name="lowrank_first",
        compiler_params=grant(14),
    )(idx, *ranks, *rights[:-1])
    far_products = pl.pallas_call(
        lowrank_last_kernel,
        out_shape=blocks,
        in_specs=[VMEM] * 3,
        out_specs=[VMEM] * (nf // 2),
        name="lowrank_last",
            compiler_params=grant(10),
    )(first, columns, rights[-1])
    near_products = pl.pallas_call(
        functools.partial(lowrank_kernel, nf, nt, near_slots),
        out_shape=blocks,
        in_specs=[SMEM] + [VMEM] * (nt + nf),
        out_specs=[VMEM] * (nf // 2),
        scratch_shapes=scratch,
        name="lowrank_near",
            compiler_params=grant(14),
    )(idx, *ranks, *rights)
    pieces = [near_products[0]]
    pieces += [move(near_products[k], df=k) for k in near_slots[1:]]
    pieces += [move(far_products[k - far[0]], df=k) for k in far]

    support = (count, share, BLK)
    outs = pl.pallas_call(
        functools.partial(final_kernel, nf),
        out_shape=[
            jax.ShapeDtypeStruct((rows, width), BF16),
            jax.ShapeDtypeStruct((rows, width), BF16),
            jax.ShapeDtypeStruct((2,) + support, F32),
        ]
        + [jax.ShapeDtypeStruct((2,) + support, BF16)] * (nz - 1),
        in_specs=[SMEM] * 3 + [VMEM] * (nf + 3),
        out_specs=[VMEM] * (nz + 2),
        scratch_shapes=[
            pltpu.VMEM((rows, width), BF16),
            pltpu.VMEM((nz, 2) + support, F32),
            pltpu.VMEM((nz, 2) + support, BF16),
        ],
        name="hidden_and_up_grads",
            compiler_params=grant(24),
    )(idx, up_rows, up_cols - base, tokens, grad_hidden, sparse, *pieces)
    hidden, dpre_gate, up_keep, *up_sends = outs
    gate_keep, gate_send = pl.pallas_call(
        functools.partial(gate_grads_kernel, nf),
        out_shape=[
            jax.ShapeDtypeStruct((nz,) + support, F32),
            jax.ShapeDtypeStruct((nz,) + support, BF16),
        ],
        in_specs=[SMEM] * 3 + [VMEM] * 2,
        out_specs=[VMEM] * 2,
        name="gate_grads",
        compiler_params=grant(10),
    )(idx, gate_rows, gate_cols - base, tokens, dpre_gate)

    up_sum = up_keep
    for j in range(1, nz):
        up_sum = up_sum + move(up_sends[j - 1], df=2 * j).astype(F32)
    gate_got = move(gate_send, df=1)
    gate_total, *gate_sums = pl.pallas_call(
        gate_add_kernel,
        out_shape=[jax.ShapeDtypeStruct(support, F32)]
        + [jax.ShapeDtypeStruct(support, BF16)] * (nz - 1),
        in_specs=[VMEM] * 2,
        out_specs=[VMEM] * nz,
        name="gate_add",
        compiler_params=grant(6),
    )(gate_keep, gate_got)
    for j in range(1, nz):
        gate_total = gate_total + move(gate_sums[j - 1], df=2 * j).astype(F32)
    up_here = jnp.where(x == 0, up_sum[0], up_sum[1])
    up_there = jnp.where(x == 0, up_sum[1], up_sum[0]).astype(BF16)
    up_total = up_here + move(up_there, df=1).astype(F32)
    return hidden, gate_total.reshape(count, share * BLK), up_total.reshape(count, share * BLK)


def placed(mesh, axes, step):
    fsdp, tp = axes
    both = P(fsdp, tp)
    swapped = P(tp, fsdp)
    return jax.shard_map(
        step,
        mesh=mesh,
        in_specs=(P(fsdp, None),) + (both, both, swapped, P(tp), P(tp)) * 2 + (both,),
        out_specs=(both, swapped, swapped),
        check_vma=False,
    )


def solution(mesh):
    nf, nt = mesh.shape["fsdp"], mesh.shape["tp"]

    def step(*args):
        width = args[2].shape[1] // nt
        if nf == 8 and nt == 4 and width % (BLK * (nf // 2)) == 0:
            split = Mesh(mesh.devices.reshape(nf // 2, 2, 2, 2), AXES)

            def body(*local):
                return exchange_device(mesh, *local)

            return placed(split, (("z", "x"), ("y", "c")), body)(*args)
        return placed(mesh, ("fsdp", "tp"), on_device)(*args)

    return step
```

```python
import functools

import jax
import jax.numpy as jnp
from jax import lax
from jax.experimental import pallas as pl
from jax.experimental.pallas import tpu as pltpu
from jax.sharding import Mesh
from jax.sharding import PartitionSpec as P

BLK = 128


def support_forward(tokens, blocks, rows, cols_local, col_blocks):
    width = tokens.shape[1] // BLK
    sources = tokens.reshape(tokens.shape[0], width, BLK)[:, rows, :]
    parts = jnp.einsum("tkb,kbc->tkc", sources, blocks, preferred_element_type=jnp.float32)
    placed = (
        jnp.zeros((tokens.shape[0], col_blocks, BLK), jnp.float32).at[:, cols_local, :].add(parts)
    )
    return (placed.reshape(tokens.shape[0], col_blocks * BLK), sources)


def value_terms(sources_gate, dpre_gate, local_gate, sources_up, dpre_up, local_up, col_blocks):
    picked_gate = dpre_gate.reshape(dpre_gate.shape[0], col_blocks, BLK)[:, local_gate, :]
    picked_up = dpre_up.reshape(dpre_up.shape[0], col_blocks, BLK)[:, local_up, :]
    value_gate = jnp.einsum(
        "tkb,tkc->kbc", sources_gate, picked_gate, preferred_element_type=jnp.float32
    )
    value_up = jnp.einsum("tkb,tkc->kbc", sources_up, picked_up, preferred_element_type=jnp.float32)
    return (
        value_gate.reshape(value_gate.shape[0], BLK * BLK),
        value_up.reshape(value_up.shape[0], BLK * BLK),
    )


def on_device(
    tokens,
    gate_left,
    gate_right,
    gate_values,
    gate_rows,
    gate_cols,
    up_left,
    up_right,
    up_values,
    up_rows,
    up_cols,
    grad_hidden,
):
    left_gate, left_up = (
        lax.all_gather(gate_left, "fsdp", axis=0, tiled=True),
        lax.all_gather(up_left, "fsdp", axis=0, tiled=True),
    )
    rank_gate = jnp.dot(tokens, left_gate, preferred_element_type=jnp.float32).astype(jnp.bfloat16)
    rank_up = jnp.dot(tokens, left_up, preferred_element_type=jnp.float32).astype(jnp.bfloat16)
    full_gate, full_up = (
        lax.all_gather(rank_gate, "tp", axis=1, tiled=True),
        lax.all_gather(rank_up, "tp", axis=1, tiled=True),
    )
    flat_gate, flat_up = (
        lax.all_gather(gate_values, "fsdp", axis=1, tiled=True),
        lax.all_gather(up_values, "fsdp", axis=1, tiled=True),
    )
    blocks_gate = flat_gate.reshape(flat_gate.shape[0], BLK, BLK)
    blocks_up = flat_up.reshape(flat_up.shape[0], BLK, BLK)
    right_gate = lax.all_gather(gate_right, "fsdp", axis=0, tiled=True)
    right_up = lax.all_gather(up_right, "fsdp", axis=0, tiled=True)
    col_blocks = right_gate.shape[1] // BLK
    col_base = lax.axis_index("tp") * col_blocks
    local_gate = gate_cols - col_base
    local_up = up_cols - col_base
    sparse_gate, sources_gate = support_forward(
        tokens, blocks_gate, gate_rows, local_gate, col_blocks
    )
    sparse_up, sources_up = support_forward(tokens, blocks_up, up_rows, local_up, col_blocks)
    pre_gate = jnp.dot(full_gate, right_gate, preferred_element_type=jnp.float32) + sparse_gate
    pre_up = jnp.dot(full_up, right_up, preferred_element_type=jnp.float32) + sparse_up
    sigma = jax.nn.sigmoid(pre_gate)
    silu = pre_gate * sigma
    upstream = grad_hidden.astype(jnp.float32)
    dpre_gate = (upstream * pre_up * sigma * (1.0 + pre_gate * (1.0 - sigma))).astype(jnp.bfloat16)
    dpre_up = (upstream * silu).astype(jnp.bfloat16)
    hidden = (silu * pre_up).astype(jnp.bfloat16)
    value_gate, value_up = value_terms(
        sources_gate, dpre_gate, local_gate, sources_up, dpre_up, local_up, col_blocks
    )
    grad_gate_values, grad_up_values = (
        lax.psum_scatter(value_gate, "fsdp", scatter_dimension=1, tiled=True),
        lax.psum_scatter(value_up, "fsdp", scatter_dimension=1, tiled=True),
    )
    return (hidden, grad_gate_values, grad_up_values)


ANY = pl.BlockSpec(memory_space=pl.ANY)
VMEM = pl.BlockSpec(memory_space=pltpu.VMEM)
SMEM = pl.BlockSpec(memory_space=pltpu.SMEM)
BF16, F32 = jnp.bfloat16, jnp.float32
AXES = ("z", "x", "y", "c")


def grant(mib):
    return pltpu.CompilerParams(vmem_limit_bytes=mib << 20)


def at(start, size):
    return pl.ds(pl.multiple_of(start, BLK), size)


def run_copies(pairs, sems):
    copies = [pltpu.make_async_copy(s, d, sems.at[i]) for i, (s, d) in enumerate(pairs)]
    for copy in copies:
        copy.start()
    return copies


def partial_kernel(nz, idx, tokens, *refs):
    n = nz - 1
    quarters, (left_g, left_u, recv_g, recv_u) = refs[: 4 * n], refs[4 * n : 4 * nz]
    own_out, outs = refs[4 * nz], refs[4 * nz + 1 : 5 * nz]
    left, toks = refs[5 * nz :]
    z, x, c, y = idx[0], idx[1], idx[2], idx[5]
    depth, width = left_g.shape
    left[x, :, :width], left[x, :, width:] = left_g[...], left_u[...]
    left[1 - x, :, :width], left[1 - x, :, width:] = recv_g[...], recv_u[...]
    toks[0] = tokens[:, at(z * 2 * depth, 2 * depth)]
    quarter = depth // 2
    for i, (dc, dy) in enumerate(((0, 0), (0, 1), (1, 0), (1, 1))):
        start = (c ^ dc) * depth + (y ^ dy) * quarter
        for j in range(1, nz):
            toks[j, :, at(start, quarter)] = quarters[i * n + j - 1][...]
    weights = left[...].reshape(2 * depth, 2 * width)
    rows = toks.shape[1]
    total = jnp.dot(
        toks[...].reshape(nz * rows, 2 * depth), weights, preferred_element_type=F32
    )
    own_out[...] = total[:rows]
    for j in range(1, nz):
        outs[j - 1][...] = total[j * rows : (j + 1) * rows].astype(BF16)


def rank_round_kernel(own, *refs):
    others, out = refs[:-1], refs[-1]
    total = own[...]
    for other in others:
        total = total + other[...].astype(F32)
    width = out.shape[2]
    for k in range(out.shape[0]):
        out[k] = total[:, k % 2 * width : (k % 2 + 1) * width].astype(BF16)


def load_ranks(nf, slots, idx, ranks, rank):
    f, t = idx[3], idx[4]
    depth = rank.shape[2] // nf
    parts = ranks[0].shape[2] // depth
    for s, source in enumerate(ranks):
        for h in range(parts):
            lanes = at((f ^ ((t ^ s) * parts + h)) * depth, depth)
            for i, m in enumerate(slots):
                rank[i, :, lanes] = source[f ^ m, :, h * depth : (h + 1) * depth]


def product(rank, rights):
    count, rows, _ = rank.shape
    weights = jnp.concatenate([right[...] for right in rights], axis=0)
    lhs = rank[:, :, : weights.shape[0]].reshape(count * rows, weights.shape[0])
    return jnp.dot(lhs, weights, preferred_element_type=F32)


def lowrank_kernel(nf, nt, slots, idx, *refs):
    ranks, rights = refs[:nt], refs[nt : nt + nf]
    outs, rank = refs[nt + nf : nt + nf + len(slots)], refs[-1]
    load_ranks(nf, slots, idx, ranks, rank)
    total = product(rank, rights)
    rows = rank.shape[1]
    for i in range(len(slots)):
        outs[i][...] = total[i * rows : (i + 1) * rows].astype(BF16)


def lowrank_first_kernel(nf, nt, slots, idx, *refs):
    ranks, rights = refs[:nt], refs[nt : nt + nf - 1]
    total, columns, rank = refs[nt + nf - 1 :]
    load_ranks(nf, slots, idx, ranks, rank)
    total[...] = product(rank, rights)
    columns[...] = rank[:, :, -columns.shape[1] :].reshape(columns.shape)


def lowrank_last_kernel(total, columns, right, *outs):
    rows = outs[0].shape[0]
    value = total[...] + jnp.dot(columns[...], right[...], preferred_element_type=F32)
    for i, out in enumerate(outs):
        out[...] = value[i * rows : (i + 1) * rows].astype(BF16)


def sparse_kernel(nf, idx, gate_rows, gate_cols, up_rows, up_cols, tokens, *refs):
    values, out, blocks, sems = refs[:nf], refs[nf], refs[nf + 1], refs[nf + 2]
    z, f = idx[0], idx[3]
    inner = jnp.logical_or(z == 1, z == 2)
    across = jnp.where(inner, 6, 4)
    slots = [0, 1, 2, 3, across, across + 1, 10 - across, 11 - across]
    copies = run_copies([(v, blocks.at[:, f ^ k]) for v, k in zip(values, slots)], sems)
    out[...] = jnp.zeros_like(out)
    for copy in copies:
        copy.wait()
    count = gate_rows.shape[0]
    for p, (rows, cols) in enumerate(((gate_rows, gate_cols), (up_rows, up_cols))):

        def step(k, carry, p=p, rows=rows, cols=cols):
            source = tokens[:, at(rows[k] * BLK, BLK)]
            block = blocks[p * count + k].reshape(BLK, BLK)
            here = at(cols[k] * BLK, BLK)
            out[p, :, here] += jnp.dot(source, block, preferred_element_type=F32)
            return carry

        lax.fori_loop(0, count, step, 0, unroll=True)


def support_grads(nf, tokens, dpre, rows, cols, k):
    source = tokens[:, at(rows[k] * BLK, BLK)]
    picked = dpre[:, at(cols[k] * BLK, BLK)]
    value = lax.dot_general(source, picked, (((0,), (0,)), ((), ())), preferred_element_type=F32)
    return value.reshape(nf // 2, 2, BLK // nf, BLK)


def final_kernel(nf, idx, up_rows, up_cols, tokens, grad, sparse, *refs):
    nz = nf // 2
    pieces = refs[:nf]
    hidden, dpre_gate, up_keep = refs[nf : nf + 3]
    up_sends = refs[nf + 3 : nf + 2 + nz]
    dpre_up, keep, send = refs[nf + 2 + nz :]
    z, x = idx[0], idx[1]
    rows, width = pieces[0].shape
    tall = rows // 2
    for j in range(nz):
        mine, other = pieces[2 * j], pieces[2 * j + 1]

        def chunk(i, carry, j=j, mine=mine, other=other):
            down = pl.ds(pl.multiple_of(i % 2 * tall, tall), tall)
            local = at(i // 2 * BLK, BLK)
            here = at((z ^ j) * width + i // 2 * BLK, BLK)
            a, b = mine[down, local].astype(F32), other[down, local].astype(F32)
            gate = jnp.where(x == 0, a, b) + sparse[0, down, here]
            up = jnp.where(x == 0, b, a) + sparse[1, down, here]
            sigma = jax.nn.sigmoid(gate)
            silu = gate * sigma
            upstream = grad[down, here].astype(F32)
            slope = upstream * up * sigma * (1.0 + gate * (1.0 - sigma))
            dpre_gate[down, here] = slope.astype(BF16)
            dpre_up[down, here] = (upstream * silu).astype(BF16)
            hidden[down, here] = (silu * up).astype(BF16)
            return carry

        lax.fori_loop(0, 2 * width // BLK, chunk, 0, unroll=True)

    def step(k, carry):
        value = support_grads(nf, tokens, dpre_up, up_rows, up_cols, k)
        for j in range(nz):
            keep[z ^ j, :, k] = value[j]
            send[z ^ j, :, k] = value[j].astype(BF16)
        return carry

    lax.fori_loop(0, up_rows.shape[0], step, 0, unroll=True)
    up_keep[...] = keep[0]
    for j in range(1, nz):
        up_sends[j - 1][...] = send[j]


def gate_grads_kernel(nf, idx, rows, cols, tokens, dpre, keep_out, send_out):
    z, x = idx[0], idx[1]

    def step(k, carry):
        value = support_grads(nf, tokens, dpre, rows, cols, k)
        keep = jnp.where(x == 0, value[:, 0], value[:, 1])
        other = jnp.where(x == 0, value[:, 1], value[:, 0]).astype(BF16)
        for j in range(nf // 2):
            keep_out[z ^ j, k] = keep[j]
            send_out[z ^ j, k] = other[j]
        return carry

    lax.fori_loop(0, rows.shape[0], step, 0, unroll=True)


def gate_add_kernel(keep, got, own, *sends):
    own[...] = keep[0] + got[0].astype(F32)
    for j, send in enumerate(sends, 1):
        send[...] = (keep[j] + got[j].astype(F32)).astype(BF16)


def exchange_device(
    mesh,
    tokens,
    gate_left,
    gate_right,
    gate_values,
    gate_rows,
    gate_cols,
    up_left,
    up_right,
    up_values,
    up_rows,
    up_cols,
    grad_hidden,
):
    nf, nt = mesh.shape["fsdp"], mesh.shape["tp"]
    nz = nf // 2
    rows, width = tokens.shape[0], gate_right.shape[1]
    depth, slice_width = gate_left.shape
    cols = width // nz
    count = gate_values.shape[0]
    share = BLK // nf
    z, x, c = lax.axis_index("z"), lax.axis_index("x"), lax.axis_index("c")
    y = lax.axis_index("y")
    f, t = 2 * z + x, 2 * y + c
    idx = jnp.stack([z, x, c, f, t, y]).astype(jnp.int32)

    def move(value, df=0, dt=0, only=range(nf)):
        pairs = [(i, i ^ (df * nt + dt)) for i in range(nf * nt) if i // (2 * nt) in only]
        return lax.ppermute(value, AXES, pairs)

    quarter = depth // 2
    fetched = [
        lax.dynamic_slice(
            tokens, (0, (z ^ j) * 2 * depth + c * depth + y * quarter), (rows, quarter)
        )
        for j in range(1, nz)
    ]
    fetched = [move(part, df=2 * j) for j, part in enumerate(fetched, 1)]
    recv_g, recv_u = move(gate_left, df=1), move(up_left, df=1)
    across_y = [move(part, dt=2) for part in fetched]
    half = [*fetched, *across_y]
    half += [move(part, dt=1) for part in half]
    sums = pl.pallas_call(
        functools.partial(partial_kernel, nz),
        out_shape=[jax.ShapeDtypeStruct((rows, 2 * slice_width), F32)]
        + [jax.ShapeDtypeStruct((rows, 2 * slice_width), BF16)] * (nz - 1),
        in_specs=[SMEM] + [VMEM] * (4 * nz + 1),
        out_specs=[VMEM] * nz,
        scratch_shapes=[
            pltpu.VMEM((2, depth, 2 * slice_width), BF16),
            pltpu.VMEM((nz, rows, 2 * depth), BF16),
        ],
        name="rank_partial",
            compiler_params=grant(10),
    )(idx, tokens, *half, gate_left, up_left, recv_g, recv_u)
    got = [move(sums[j], df=2 * j) for j in range(1, nz)]
    for_f = pl.pallas_call(
        rank_round_kernel,
        out_shape=jax.ShapeDtypeStruct((nf, rows, slice_width), BF16),
        in_specs=[VMEM] * nz,
        out_specs=VMEM,
        name="rr11",
        compiler_params=grant(4),
    )(sums[0], *got)
    stack = lax.all_to_all(for_f, ("z", "x"), 0, 0, tiled=True)
    ranks = [stack, move(stack, dt=1), move(stack, dt=2)]
    ranks.append(move(ranks[2], dt=1))

    rights = []
    later_gate, later_up, _ = lax.optimization_barrier((gate_right, up_right, fetched[0]))
    for k in range(nf):
        gate_k, up_k = (gate_right, up_right) if k in (4, 5) else (later_gate, later_up)
        start = (0, (z ^ (k // 2)) * cols)
        size = (gate_right.shape[0], cols)
        rights.append(
            jnp.where(
                (x ^ (k % 2)) == 0,
                lax.dynamic_slice(gate_k, start, size),
                lax.dynamic_slice(up_k, start, size),
            )
        )
    rights = [rights[0]] + [move(rights[k], df=k) for k in range(1, nf)]

    own_values = jnp.concatenate([gate_values, up_values], 0).reshape(2 * count, share, BLK)
    near = move(own_values, df=2)
    inner = (z == 1) | (z == 2)
    from_across = [
        jnp.where(inner, got, move(got, df=2, only=(1, 2)))
        for got in (move(v, df=6, only=(1, 2)) for v in (own_values, near))
    ]
    values = [own_values, move(own_values, df=1)]
    values += [near, move(near, df=1)]
    for v in from_across:
        values += [v, move(v, df=1)]
    base = t * (width // BLK)
    index = (idx, gate_rows, gate_cols - base, up_rows, up_cols - base)
    sparse = pl.pallas_call(
        functools.partial(sparse_kernel, nf),
        out_shape=jax.ShapeDtypeStruct((2, rows, width), F32),
        in_specs=[SMEM] * 5 + [VMEM] + [ANY] * nf,
        out_specs=VMEM,
        scratch_shapes=[
            pltpu.VMEM((2 * count, nf, share, BLK), BF16),
            pltpu.SemaphoreType.DMA((nf,)),
        ],
        name="sparse_forward",
        compiler_params=grant(14),
    )(*index, tokens, *values)

    depth_k, far, near_slots = gate_right.shape[0], range(nf // 2, nf), range(nf // 2)
    scratch = [pltpu.VMEM((nf // 2, rows, nt * slice_width), BF16)]
    blocks = [jax.ShapeDtypeStruct((rows, cols), BF16)] * (nf // 2)
    first, columns = pl.pallas_call(
        functools.partial(lowrank_first_kernel, nf, nt, far),
        out_shape=[
            jax.ShapeDtypeStruct((nf // 2 * rows, cols), F32),
            jax.ShapeDtypeStruct((nf // 2 * rows, depth_k), BF16),
        ],
        in_specs=[SMEM] + [VMEM] * (nt + nf - 1),
        out_specs=[VMEM] * 2,
        scratch_shapes=scratch,
        name="lf28",
        compiler_params=grant(14),
    )(idx, *ranks, *rights[:-1])
    far_products = pl.pallas_call(
        lowrank_last_kernel,
        out_shape=blocks,
        in_specs=[VMEM] * 3,
        out_specs=[VMEM] * (nf // 2),
        name="lowrank_last",
            compiler_params=grant(10),
    )(first, columns, rights[-1])
    near_products = pl.pallas_call(
        functools.partial(lowrank_kernel, nf, nt, near_slots),
        out_shape=blocks,
        in_specs=[SMEM] + [VMEM] * (nt + nf),
        out_specs=[VMEM] * (nf // 2),
        scratch_shapes=scratch,
        name="lowrank_near",
            compiler_params=grant(14),
    )(idx, *ranks, *rights)
    pieces = [near_products[0]]
    pieces += [move(near_products[k], df=k) for k in near_slots[1:]]
    pieces += [move(far_products[k - far[0]], df=k) for k in far]

    support = (count, share, BLK)
    outs = pl.pallas_call(
        functools.partial(final_kernel, nf),
        out_shape=[
            jax.ShapeDtypeStruct((rows, width), BF16),
            jax.ShapeDtypeStruct((rows, width), BF16),
            jax.ShapeDtypeStruct((2,) + support, F32),
        ]
        + [jax.ShapeDtypeStruct((2,) + support, BF16)] * (nz - 1),
        in_specs=[SMEM] * 3 + [VMEM] * (nf + 3),
        out_specs=[VMEM] * (nz + 2),
        scratch_shapes=[
            pltpu.VMEM((rows, width), BF16),
            pltpu.VMEM((nz, 2) + support, F32),
            pltpu.VMEM((nz, 2) + support, BF16),
        ],
        name="hidden_and_up_grads",
            compiler_params=grant(24),
    )(idx, up_rows, up_cols - base, tokens, grad_hidden, sparse, *pieces)
    hidden, dpre_gate, up_keep, *up_sends = outs
    gate_keep, gate_send = pl.pallas_call(
        functools.partial(gate_grads_kernel, nf),
        out_shape=[
            jax.ShapeDtypeStruct((nz,) + support, F32),
            jax.ShapeDtypeStruct((nz,) + support, BF16),
        ],
        in_specs=[SMEM] * 3 + [VMEM] * 2,
        out_specs=[VMEM] * 2,
        name="gg27",
        compiler_params=grant(10),
    )(idx, gate_rows, gate_cols - base, tokens, dpre_gate)

    up_sum = up_keep
    for j in range(1, nz):
        up_sum = up_sum + move(up_sends[j - 1], df=2 * j).astype(F32)
    gate_got = move(gate_send, df=1)
    gate_total, *gate_sums = pl.pallas_call(
        gate_add_kernel,
        out_shape=[jax.ShapeDtypeStruct(support, F32)]
        + [jax.ShapeDtypeStruct(support, BF16)] * (nz - 1),
        in_specs=[VMEM] * 2,
        out_specs=[VMEM] * nz,
        name="ga26",
        compiler_params=grant(6),
    )(gate_keep, gate_got)
    for j in range(1, nz):
        gate_total = gate_total + move(gate_sums[j - 1], df=2 * j).astype(F32)
    up_here = jnp.where(x == 0, up_sum[0], up_sum[1])
    up_there = jnp.where(x == 0, up_sum[1], up_sum[0]).astype(BF16)
    up_total = up_here + move(up_there, df=1).astype(F32)
    return hidden, gate_total.reshape(count, share * BLK), up_total.reshape(count, share * BLK)


def placed(mesh, axes, step):
    fsdp, tp = axes
    both = P(fsdp, tp)
    swapped = P(tp, fsdp)
    return jax.shard_map(
        step,
        mesh=mesh,
        in_specs=(P(fsdp, None),) + (both, both, swapped, P(tp), P(tp)) * 2 + (both,),
        out_specs=(both, swapped, swapped),
        check_vma=False,
    )


def solution(mesh):
    nf, nt = mesh.shape["fsdp"], mesh.shape["tp"]

    def step(*args):
        width = args[2].shape[1] // nt
        if nf == 8 and nt == 4 and width % (BLK * (nf // 2)) == 0:
            split = Mesh(mesh.devices.reshape(nf // 2, 2, 2, 2), AXES)

            def body(*local):
                return exchange_device(mesh, *local)

            return placed(split, (("z", "x"), ("y", "c")), body)(*args)
        return placed(mesh, ("fsdp", "tp"), on_device)(*args)

    return step
```

```python
import functools

import jax
import jax.numpy as jnp
from jax import lax
from jax.experimental import pallas as pl
from jax.experimental.pallas import tpu as pltpu
from jax.sharding import Mesh
from jax.sharding import PartitionSpec as P

BLK = 128


def support_forward(tokens, blocks, rows, cols_local, col_blocks):
    width = tokens.shape[1] // BLK
    sources = tokens.reshape(tokens.shape[0], width, BLK)[:, rows, :]
    parts = jnp.einsum("tkb,kbc->tkc", sources, blocks, preferred_element_type=jnp.float32)
    placed = (
        jnp.zeros((tokens.shape[0], col_blocks, BLK), jnp.float32).at[:, cols_local, :].add(parts)
    )
    return (placed.reshape(tokens.shape[0], col_blocks * BLK), sources)


def value_terms(sources_gate, dpre_gate, local_gate, sources_up, dpre_up, local_up, col_blocks):
    picked_gate = dpre_gate.reshape(dpre_gate.shape[0], col_blocks, BLK)[:, local_gate, :]
    picked_up = dpre_up.reshape(dpre_up.shape[0], col_blocks, BLK)[:, local_up, :]
    value_gate = jnp.einsum(
        "tkb,tkc->kbc", sources_gate, picked_gate, preferred_element_type=jnp.float32
    )
    value_up = jnp.einsum("tkb,tkc->kbc", sources_up, picked_up, preferred_element_type=jnp.float32)
    return (
        value_gate.reshape(value_gate.shape[0], BLK * BLK),
        value_up.reshape(value_up.shape[0], BLK * BLK),
    )


def on_device(
    tokens,
    gate_left,
    gate_right,
    gate_values,
    gate_rows,
    gate_cols,
    up_left,
    up_right,
    up_values,
    up_rows,
    up_cols,
    grad_hidden,
):
    left_gate, left_up = (
        lax.all_gather(gate_left, "fsdp", axis=0, tiled=True),
        lax.all_gather(up_left, "fsdp", axis=0, tiled=True),
    )
    rank_gate = jnp.dot(tokens, left_gate, preferred_element_type=jnp.float32).astype(jnp.bfloat16)
    rank_up = jnp.dot(tokens, left_up, preferred_element_type=jnp.float32).astype(jnp.bfloat16)
    full_gate, full_up = (
        lax.all_gather(rank_gate, "tp", axis=1, tiled=True),
        lax.all_gather(rank_up, "tp", axis=1, tiled=True),
    )
    flat_gate, flat_up = (
        lax.all_gather(gate_values, "fsdp", axis=1, tiled=True),
        lax.all_gather(up_values, "fsdp", axis=1, tiled=True),
    )
    blocks_gate = flat_gate.reshape(flat_gate.shape[0], BLK, BLK)
    blocks_up = flat_up.reshape(flat_up.shape[0], BLK, BLK)
    right_gate = lax.all_gather(gate_right, "fsdp", axis=0, tiled=True)
    right_up = lax.all_gather(up_right, "fsdp", axis=0, tiled=True)
    col_blocks = right_gate.shape[1] // BLK
    col_base = lax.axis_index("tp") * col_blocks
    local_gate = gate_cols - col_base
    local_up = up_cols - col_base
    sparse_gate, sources_gate = support_forward(
        tokens, blocks_gate, gate_rows, local_gate, col_blocks
    )
    sparse_up, sources_up = support_forward(tokens, blocks_up, up_rows, local_up, col_blocks)
    pre_gate = jnp.dot(full_gate, right_gate, preferred_element_type=jnp.float32) + sparse_gate
    pre_up = jnp.dot(full_up, right_up, preferred_element_type=jnp.float32) + sparse_up
    sigma = jax.nn.sigmoid(pre_gate)
    silu = pre_gate * sigma
    upstream = grad_hidden.astype(jnp.float32)
    dpre_gate = (upstream * pre_up * sigma * (1.0 + pre_gate * (1.0 - sigma))).astype(jnp.bfloat16)
    dpre_up = (upstream * silu).astype(jnp.bfloat16)
    hidden = (silu * pre_up).astype(jnp.bfloat16)
    value_gate, value_up = value_terms(
        sources_gate, dpre_gate, local_gate, sources_up, dpre_up, local_up, col_blocks
    )
    grad_gate_values, grad_up_values = (
        lax.psum_scatter(value_gate, "fsdp", scatter_dimension=1, tiled=True),
        lax.psum_scatter(value_up, "fsdp", scatter_dimension=1, tiled=True),
    )
    return (hidden, grad_gate_values, grad_up_values)


ANY = pl.BlockSpec(memory_space=pl.ANY)
VMEM = pl.BlockSpec(memory_space=pltpu.VMEM)
HBM = pl.BlockSpec(memory_space=pltpu.HBM)
SMEM = pl.BlockSpec(memory_space=pltpu.SMEM)
BF16, F32 = jnp.bfloat16, jnp.float32
AXES = ("z", "x", "y", "c")


def grant(mib):
    return pltpu.CompilerParams(vmem_limit_bytes=mib << 20)


def at(start, size):
    return pl.ds(pl.multiple_of(start, BLK), size)


def run_copies(pairs, sems):
    copies = [pltpu.make_async_copy(s, d, sems.at[i]) for i, (s, d) in enumerate(pairs)]
    for copy in copies:
        copy.start()
    return copies


def partial_kernel(nz, idx, tokens, *refs):
    n = nz - 1
    quarters, (left_g, left_u, recv_g, recv_u) = refs[: 4 * n], refs[4 * n : 4 * nz]
    own_out, outs = refs[4 * nz], refs[4 * nz + 1 : 5 * nz]
    left, toks, sems = refs[5 * nz :]
    z, x, c, y = idx[0], idx[1], idx[2], idx[5]
    depth, width = left_g.shape
    pairs = [
        (left_g, left.at[x, :, pl.ds(0, width)]),
        (left_u, left.at[x, :, pl.ds(width, width)]),
        (tokens.at[:, at(z * 2 * depth, 2 * depth)], toks.at[0]),
    ]
    copies = run_copies(pairs, sems)
    left[1 - x, :, :width], left[1 - x, :, width:] = recv_g[...], recv_u[...]
    quarter = depth // 2
    for i, (dc, dy) in enumerate(((0, 0), (0, 1), (1, 0), (1, 1))):
        start = (c ^ dc) * depth + (y ^ dy) * quarter
        for j in range(1, nz):
            toks[j, :, at(start, quarter)] = quarters[i * n + j - 1][...]
    for copy in copies:
        copy.wait()
    weights = left[...].reshape(2 * depth, 2 * width)
    rows = toks.shape[1]
    total = jnp.dot(
        toks[...].reshape(nz * rows, 2 * depth), weights, preferred_element_type=F32
    )
    own_out[...] = total[:rows]
    for j in range(1, nz):
        outs[j - 1][...] = total[j * rows : (j + 1) * rows].astype(BF16)


def rank_round_kernel(own, *refs):
    others, out = refs[:-1], refs[-1]
    total = own[...]
    for other in others:
        total = total + other[...].astype(F32)
    width = out.shape[2]
    for k in range(out.shape[0]):
        out[k] = total[:, k % 2 * width : (k % 2 + 1) * width].astype(BF16)


def load_ranks(nf, slots, idx, ranks, rank):
    f, t = idx[3], idx[4]
    depth = rank.shape[2] // nf
    parts = ranks[0].shape[2] // depth
    for s, source in enumerate(ranks):
        for h in range(parts):
            lanes = at((f ^ ((t ^ s) * parts + h)) * depth, depth)
            for i, m in enumerate(slots):
                rank[i, :, lanes] = source[f ^ m, :, h * depth : (h + 1) * depth]


def product(rank, rights):
    count, rows, _ = rank.shape
    weights = jnp.concatenate([right[...] for right in rights], axis=0)
    lhs = rank[:, :, : weights.shape[0]].reshape(count * rows, weights.shape[0])
    return jnp.dot(lhs, weights, preferred_element_type=F32)


def lowrank_kernel(nf, nt, slots, idx, *refs):
    ranks, rights = refs[:nt], refs[nt : nt + nf]
    outs, rank = refs[nt + nf : nt + nf + len(slots)], refs[-1]
    load_ranks(nf, slots, idx, ranks, rank)
    total = product(rank, rights)
    rows = rank.shape[1]
    for i in range(len(slots)):
        outs[i][...] = total[i * rows : (i + 1) * rows].astype(BF16)


def lowrank_first_kernel(nf, nt, slots, idx, *refs):
    ranks, rights = refs[:nt], refs[nt : nt + nf - 1]
    total, columns, rank = refs[nt + nf - 1 :]
    load_ranks(nf, slots, idx, ranks, rank)
    total[...] = product(rank, rights)
    columns[...] = rank[:, :, -columns.shape[1] :].reshape(columns.shape)


def lowrank_last_kernel(total, columns, right, *outs):
    rows = outs[0].shape[0]
    value = total[...] + jnp.dot(columns[...], right[...], preferred_element_type=F32)
    for i, out in enumerate(outs):
        out[...] = value[i * rows : (i + 1) * rows].astype(BF16)


def sparse_kernel(nf, idx, gate_rows, gate_cols, up_rows, up_cols, tokens, *refs):
    values, out, blocks, sems = refs[:nf], refs[nf], refs[nf + 1], refs[nf + 2]
    z, f = idx[0], idx[3]
    inner = jnp.logical_or(z == 1, z == 2)
    across = jnp.where(inner, 6, 4)
    slots = [0, 1, 2, 3, across, across + 1, 10 - across, 11 - across]
    copies = run_copies([(v, blocks.at[:, f ^ k]) for v, k in zip(values, slots)], sems)
    out[...] = jnp.zeros_like(out)
    for copy in copies:
        copy.wait()
    count = gate_rows.shape[0]
    for p, (rows, cols) in enumerate(((gate_rows, gate_cols), (up_rows, up_cols))):

        def step(k, carry, p=p, rows=rows, cols=cols):
            source = tokens[:, at(rows[k] * BLK, BLK)]
            block = blocks[p * count + k].reshape(BLK, BLK)
            here = at(cols[k] * BLK, BLK)
            out[p, :, here] += jnp.dot(source, block, preferred_element_type=F32)
            return carry

        lax.fori_loop(0, count, step, 0, unroll=True)


def support_grads(nf, tokens, dpre, rows, cols, k):
    source = tokens[:, at(rows[k] * BLK, BLK)]
    picked = dpre[:, at(cols[k] * BLK, BLK)]
    value = lax.dot_general(source, picked, (((0,), (0,)), ((), ())), preferred_element_type=F32)
    return value.reshape(nf // 2, 2, BLK // nf, BLK)


def final_kernel(nf, idx, up_rows, up_cols, tokens, grad, sparse, *refs):
    nz = nf // 2
    pieces = refs[:nf]
    hidden, dpre_gate, up_keep = refs[nf : nf + 3]
    up_sends = refs[nf + 3 : nf + 2 + nz]
    dpre_up, keep, send = refs[nf + 2 + nz :]
    z, x = idx[0], idx[1]
    rows, width = pieces[0].shape
    tall = rows // 2
    for j in range(nz):
        mine, other = pieces[2 * j], pieces[2 * j + 1]

        def chunk(i, carry, j=j, mine=mine, other=other):
            down = pl.ds(pl.multiple_of(i % 2 * tall, tall), tall)
            local = at(i // 2 * BLK, BLK)
            here = at((z ^ j) * width + i // 2 * BLK, BLK)
            a, b = mine[down, local].astype(F32), other[down, local].astype(F32)
            gate = jnp.where(x == 0, a, b) + sparse[0, down, here]
            up = jnp.where(x == 0, b, a) + sparse[1, down, here]
            sigma = jax.nn.sigmoid(gate)
            silu = gate * sigma
            upstream = grad[down, here].astype(F32)
            slope = upstream * up * sigma * (1.0 + gate * (1.0 - sigma))
            dpre_gate[down, here] = slope.astype(BF16)
            dpre_up[down, here] = (upstream * silu).astype(BF16)
            hidden[down, here] = (silu * up).astype(BF16)
            return carry

        lax.fori_loop(0, 2 * width // BLK, chunk, 0, unroll=True)

    def step(k, carry):
        value = support_grads(nf, tokens, dpre_up, up_rows, up_cols, k)
        for j in range(nz):
            keep[z ^ j, :, k] = value[j]
            send[z ^ j, :, k] = value[j].astype(BF16)
        return carry

    lax.fori_loop(0, up_rows.shape[0], step, 0, unroll=True)
    up_keep[...] = keep[0]
    for j in range(1, nz):
        up_sends[j - 1][...] = send[j]


def gate_grads_kernel(nf, idx, rows, cols, tokens, dpre, keep_out, send_out):
    z, x = idx[0], idx[1]

    def step(k, carry):
        value = support_grads(nf, tokens, dpre, rows, cols, k)
        keep = jnp.where(x == 0, value[:, 0], value[:, 1])
        other = jnp.where(x == 0, value[:, 1], value[:, 0]).astype(BF16)
        for j in range(nf // 2):
            keep_out[z ^ j, k] = keep[j]
            send_out[z ^ j, k] = other[j]
        return carry

    lax.fori_loop(0, rows.shape[0], step, 0, unroll=True)


def gate_add_kernel(keep, got, own, *sends):
    own[...] = keep[0] + got[0].astype(F32)
    for j, send in enumerate(sends, 1):
        send[...] = (keep[j] + got[j].astype(F32)).astype(BF16)


def exchange_device(
    mesh,
    tokens,
    gate_left,
    gate_right,
    gate_values,
    gate_rows,
    gate_cols,
    up_left,
    up_right,
    up_values,
    up_rows,
    up_cols,
    grad_hidden,
):
    nf, nt = mesh.shape["fsdp"], mesh.shape["tp"]
    nz = nf // 2
    rows, width = tokens.shape[0], gate_right.shape[1]
    depth, slice_width = gate_left.shape
    cols = width // nz
    count = gate_values.shape[0]
    share = BLK // nf
    z, x, c = lax.axis_index("z"), lax.axis_index("x"), lax.axis_index("c")
    y = lax.axis_index("y")
    f, t = 2 * z + x, 2 * y + c
    idx = jnp.stack([z, x, c, f, t, y]).astype(jnp.int32)

    def move(value, df=0, dt=0, only=range(nf)):
        pairs = [(i, i ^ (df * nt + dt)) for i in range(nf * nt) if i // (2 * nt) in only]
        return lax.ppermute(value, AXES, pairs)

    quarter = depth // 2
    fetched = [
        lax.dynamic_slice(
            tokens, (0, (z ^ j) * 2 * depth + c * depth + y * quarter), (rows, quarter)
        )
        for j in range(1, nz)
    ]
    fetched = [move(part, df=2 * j) for j, part in enumerate(fetched, 1)]
    recv_g, recv_u = move(gate_left, df=1), move(up_left, df=1)
    across_y = [move(part, dt=2) for part in fetched]
    half = [*fetched, *across_y]
    half += [move(part, dt=1) for part in half]
    sums = pl.pallas_call(
        functools.partial(partial_kernel, nz),
        out_shape=[jax.ShapeDtypeStruct((rows, 2 * slice_width), F32)]
        + [jax.ShapeDtypeStruct((rows, 2 * slice_width), BF16)] * (nz - 1),
        in_specs=[SMEM, HBM] + [VMEM] * (4 * nz - 4) + [HBM] * 2 + [VMEM] * 2,
        out_specs=[VMEM] * nz,
        scratch_shapes=[
            pltpu.VMEM((2, depth, 2 * slice_width), BF16),
            pltpu.VMEM((nz, rows, 2 * depth), BF16),
            pltpu.SemaphoreType.DMA((3,)),
        ],
        name="rank_partial",
            compiler_params=grant(10),
    )(idx, tokens, *half, gate_left, up_left, recv_g, recv_u)
    got = [move(sums[j], df=2 * j) for j in range(1, nz)]
    for_f = pl.pallas_call(
        rank_round_kernel,
        out_shape=jax.ShapeDtypeStruct((nf, rows, slice_width), BF16),
        in_specs=[VMEM] * nz,
        out_specs=VMEM,
        name="rr11",
        compiler_params=grant(4),
    )(sums[0], *got)
    stack = lax.all_to_all(for_f, ("z", "x"), 0, 0, tiled=True)
    ranks = [stack, move(stack, dt=1), move(stack, dt=2)]
    ranks.append(move(ranks[2], dt=1))

    rights = []
    later_gate, later_up, _ = lax.optimization_barrier((gate_right, up_right, fetched[0]))
    for k in range(nf):
        gate_k, up_k = (gate_right, up_right) if k in (4, 5) else (later_gate, later_up)
        start = (0, (z ^ (k // 2)) * cols)
        size = (gate_right.shape[0], cols)
        rights.append(
            jnp.where(
                (x ^ (k % 2)) == 0,
                lax.dynamic_slice(gate_k, start, size),
                lax.dynamic_slice(up_k, start, size),
            )
        )
    rights = [rights[0]] + [move(rights[k], df=k) for k in range(1, nf)]

    own_values = jnp.concatenate([gate_values, up_values], 0).reshape(2 * count, share, BLK)
    near = move(own_values, df=2)
    inner = (z == 1) | (z == 2)
    from_across = [
        jnp.where(inner, got, move(got, df=2, only=(1, 2)))
        for got in (move(v, df=6, only=(1, 2)) for v in (own_values, near))
    ]
    values = [own_values, move(own_values, df=1)]
    values += [near, move(near, df=1)]
    for v in from_across:
        values += [v, move(v, df=1)]
    base = t * (width // BLK)
    index = (idx, gate_rows, gate_cols - base, up_rows, up_cols - base)
    sparse = pl.pallas_call(
        functools.partial(sparse_kernel, nf),
        out_shape=jax.ShapeDtypeStruct((2, rows, width), F32),
        in_specs=[SMEM] * 5 + [VMEM] + [ANY] * nf,
        out_specs=VMEM,
        scratch_shapes=[
            pltpu.VMEM((2 * count, nf, share, BLK), BF16),
            pltpu.SemaphoreType.DMA((nf,)),
        ],
        name="sparse_forward",
        compiler_params=grant(10),
    )(*index, tokens, *values)

    depth_k, far, near_slots = gate_right.shape[0], range(nf // 2, nf), range(nf // 2)
    scratch = [pltpu.VMEM((nf // 2, rows, nt * slice_width), BF16)]
    blocks = [jax.ShapeDtypeStruct((rows, cols), BF16)] * (nf // 2)
    first, columns = pl.pallas_call(
        functools.partial(lowrank_first_kernel, nf, nt, far),
        out_shape=[
            jax.ShapeDtypeStruct((nf // 2 * rows, cols), F32),
            jax.ShapeDtypeStruct((nf // 2 * rows, depth_k), BF16),
        ],
        in_specs=[SMEM] + [VMEM] * (nt + nf - 1),
        out_specs=[VMEM] * 2,
        scratch_shapes=scratch,
        name="lf28",
        compiler_params=grant(9),
    )(idx, *ranks, *rights[:-1])
    far_products = pl.pallas_call(
        lowrank_last_kernel,
        out_shape=blocks,
        in_specs=[VMEM] * 3,
        out_specs=[VMEM] * (nf // 2),
        name="lowrank_last",
            compiler_params=grant(6),
    )(first, columns, rights[-1])
    near_products = pl.pallas_call(
        functools.partial(lowrank_kernel, nf, nt, near_slots),
        out_shape=blocks,
        in_specs=[SMEM] + [VMEM] * (nt + nf),
        out_specs=[VMEM] * (nf // 2),
        scratch_shapes=scratch,
        name="lowrank_near",
            compiler_params=grant(9),
    )(idx, *ranks, *rights)
    pieces = [near_products[0]]
    pieces += [move(near_products[k], df=k) for k in near_slots[1:]]
    pieces += [move(far_products[k - far[0]], df=k) for k in far]

    support = (count, share, BLK)
    outs = pl.pallas_call(
        functools.partial(final_kernel, nf),
        out_shape=[
            jax.ShapeDtypeStruct((rows, width), BF16),
            jax.ShapeDtypeStruct((rows, width), BF16),
            jax.ShapeDtypeStruct((2,) + support, F32),
        ]
        + [jax.ShapeDtypeStruct((2,) + support, BF16)] * (nz - 1),
        in_specs=[SMEM] * 3 + [VMEM] * (nf + 3),
        out_specs=[VMEM] * (nz + 2),
        scratch_shapes=[
            pltpu.VMEM((rows, width), BF16),
            pltpu.VMEM((nz, 2) + support, F32),
            pltpu.VMEM((nz, 2) + support, BF16),
        ],
        name="hidden_and_up_grads",
            compiler_params=grant(16),
    )(idx, up_rows, up_cols - base, tokens, grad_hidden, sparse, *pieces)
    hidden, dpre_gate, up_keep, *up_sends = outs
    gate_keep, gate_send = pl.pallas_call(
        functools.partial(gate_grads_kernel, nf),
        out_shape=[
            jax.ShapeDtypeStruct((nz,) + support, F32),
            jax.ShapeDtypeStruct((nz,) + support, BF16),
        ],
        in_specs=[SMEM] * 3 + [VMEM] * 2,
        out_specs=[VMEM] * 2,
        name="gg27",
        compiler_params=grant(8),
    )(idx, gate_rows, gate_cols - base, tokens, dpre_gate)

    up_sum = up_keep
    for j in range(1, nz):
        up_sum = up_sum + move(up_sends[j - 1], df=2 * j).astype(F32)
    gate_got = move(gate_send, df=1)
    gate_total, *gate_sums = pl.pallas_call(
        gate_add_kernel,
        out_shape=[jax.ShapeDtypeStruct(support, F32)]
        + [jax.ShapeDtypeStruct(support, BF16)] * (nz - 1),
        in_specs=[VMEM] * 2,
        out_specs=[VMEM] * nz,
        name="ga26",
        compiler_params=grant(6),
    )(gate_keep, gate_got)
    for j in range(1, nz):
        gate_total = gate_total + move(gate_sums[j - 1], df=2 * j).astype(F32)
    up_here = jnp.where(x == 0, up_sum[0], up_sum[1])
    up_there = jnp.where(x == 0, up_sum[1], up_sum[0]).astype(BF16)
    up_total = up_here + move(up_there, df=1).astype(F32)
    return hidden, gate_total.reshape(count, share * BLK), up_total.reshape(count, share * BLK)


def placed(mesh, axes, step):
    fsdp, tp = axes
    both = P(fsdp, tp)
    swapped = P(tp, fsdp)
    return jax.shard_map(
        step,
        mesh=mesh,
        in_specs=(P(fsdp, None),) + (both, both, swapped, P(tp), P(tp)) * 2 + (both,),
        out_specs=(both, swapped, swapped),
        check_vma=False,
    )


def solution(mesh):
    nf, nt = mesh.shape["fsdp"], mesh.shape["tp"]

    def step(*args):
        width = args[2].shape[1] // nt
        if nf == 8 and nt == 4 and width % (BLK * (nf // 2)) == 0:
            split = Mesh(mesh.devices.reshape(nf // 2, 2, 2, 2), AXES)

            def body(*local):
                return exchange_device(mesh, *local)

            return placed(split, (("z", "x"), ("y", "c")), body)(*args)
        return placed(mesh, ("fsdp", "tp"), on_device)(*args)

    return step
```
